32 devices in a mesh: tm: 8 (over y, x, core), space: 4 (over z).
Axes of the slice: x: 2, y: 2, z: 4, core: 2. Of those that a mesh axis runs over, the one named last changes fastest.
Arguments:
- queries: bfloat16 [16384, 1536], P(('tm', 'space')), may hold values from -6 to 6
- key_rows: bfloat16 [16384, 1536], P(('tm', 'space')), may hold values from -6 to 6
- value_rows: bfloat16 [16384, 1536], P(('tm', 'space')), may hold values from -6 to 6
- block_list: int32 [128, 8], P(('tm', 'space')), may hold values from 0 to 127, as said below
- block_count: int32 [128], P(('tm', 'space')), may hold values from 1 to 8
Outputs:
- attended: bfloat16 [16384, 1536], P(('tm', 'space'))
The draws below stay inside these ranges and needn't reach their ends.
Inputs may be any that keep to these rules, and one draw needn't show every extreme that they name: `block_list`: the candidates of query tile t, which lies in frame f = t // 16 at block p = t % 16 of the frame and in slab s = p // 4, are: the blocks of frame f with in-frame index from s * 4 - 1 to (s + 1) * 4 that lie within the frame; and, for each b from 0 to 2 and each of the frames f - 2**b and f + 2**b that lie within the clip, its blocks with in-frame index s * 4 + j where j runs over 0 to 3 with j % 2 == b % 2. Every entry of row t, padded ones included, is such a candidate, the entries of a row are distinct, and the first entry is block t itself.
All inputs are finite; a program needn't handle non-finite values.
Results may differ from the reference program's by a relative error of at most 0.0044.
Values may be sent and summed in bfloat16 or wider, within the bound.
A program may use at most 128 MiB of HBM per device.

```python
import jax
import jax.numpy as jnp
from jax import lax

HEADS = 12
HEAD = 128
D = 1536
BLOCK = 128
BLOCKS_DEV = 4
TM_BITS = 3
LIST = 8
FRAME_BLOCKS = 16
QTILES = 128
TOKENS = 16384
N_TM = 8
N_SPACE = 4


def pair_fields(key):
    key_base = jax.random.fold_in(key, 11)
    key_one, key_two = jax.random.split(key_base, 2)
    query_field = jnp.clip(jax.random.normal(key_one, (TOKENS, D), jnp.float32), -6.0, 6.0)
    key_field = jnp.clip(jax.random.normal(key_two, (TOKENS, D), jnp.float32), -6.0, 6.0)
    return (query_field, key_field)


def draw_queries(key, part):
    return pair_fields(key)[0].astype(jnp.bfloat16)


def draw_key_rows(key, part):
    return pair_fields(key)[1].astype(jnp.bfloat16)


def mask_lists(key):
    key_base = jax.random.fold_in(key, 7)
    key_one, key_two = jax.random.split(key_base, 2)
    tile_ids = jnp.arange(QTILES, dtype=jnp.int32)
    frame_ids = tile_ids // FRAME_BLOCKS
    inner_ids = tile_ids % FRAME_BLOCKS
    slab_ids = inner_ids // BLOCKS_DEV
    local_ids = inner_ids % BLOCKS_DEV
    first_block = frame_ids * FRAME_BLOCKS + slab_ids * BLOCKS_DEV
    offsets = jnp.arange(BLOCKS_DEV + 2, dtype=jnp.int32) - 1
    near_ids = first_block[:, None] + offsets[None, :]
    near_ok = ((slab_ids[:, None] > 0) | (offsets[None, :] >= 0)) & ((slab_ids[:, None] < N_SPACE - 1) | (offsets[None, :] < BLOCKS_DEV))
    own_mark = offsets[None, :] == local_ids[:, None]
    id_parts = [near_ids]
    ok_parts = [near_ok]
    own_parts = [own_mark]
    picks_base = 2 * jnp.arange(BLOCKS_DEV // 2, dtype=jnp.int32)
    for bit_index in range(TM_BITS):
        for direction in (-1, 1):
            partner_frame = frame_ids + direction * (1 << bit_index)
            frame_ok = (partner_frame >= 0) & (partner_frame < N_TM)
            safe_frame = jnp.clip(partner_frame, 0, N_TM - 1)
            band_ids = safe_frame[:, None] * FRAME_BLOCKS + slab_ids[:, None] * BLOCKS_DEV + picks_base[None, :] + bit_index % 2
            id_parts.append(band_ids)
            ok_parts.append(jnp.broadcast_to(frame_ok[:, None], band_ids.shape))
            own_parts.append(jnp.zeros(band_ids.shape, dtype=bool))
    cand_ids = jnp.concatenate(id_parts, axis=1)
    cand_ok = jnp.concatenate(ok_parts, axis=1)
    cand_own = jnp.concatenate(own_parts, axis=1)
    width_cand = cand_ids.shape[1]
    ranks = jax.random.randint(key_one, (QTILES, width_cand), 0, 1 << 20) * width_cand + jnp.arange(width_cand, dtype=jnp.int32)[None, :]
    ranks = jnp.where(cand_own, -1, jnp.where(cand_ok, ranks, 1 << 30))
    picked = jnp.argsort(ranks, axis=1, stable=True)[:, :LIST]
    lists = jnp.take_along_axis(cand_ids, picked, axis=1).astype(jnp.int32)
    counts = jax.random.randint(key_two, (QTILES,), 1, LIST + 1)
    counts = jnp.where(tile_ids % 5 == 1, 1, counts)
    counts = jnp.where(tile_ids % 3 == 0, LIST, counts).astype(jnp.int32)
    return (lists, counts)


def draw_block_list(key, part):
    return mask_lists(key)[0]


def draw_block_count(key, part):
    return mask_lists(key)[1]


def shard_levels(rng, shape, cuts, low, largest):
    factor_of, own = 1.0, jax.random.fold_in(rng, 6)
    for dim, blocks in cuts:
        heights = jnp.exp(jax.random.uniform(jax.random.fold_in(own, dim), (blocks,), jnp.float32, low / len(cuts), largest / len(cuts)))
        factor_of = factor_of * jnp.repeat(heights, shape[dim] // blocks).reshape([-1 if axis == dim else 1 for axis in range(len(shape))])
    return factor_of


def scatter_about(rng, shape, width, bound, cuts=(), kind=jnp.bfloat16):
    loudness = shard_levels(rng, shape, cuts, -0.22, 0.18) if cuts else 1.0
    values = jax.random.normal(rng, shape, jnp.float32) * width * loudness
    return jnp.minimum(jnp.maximum(values, -bound), bound).astype(kind)


def setup_inputs(seed: int = 0) -> dict:
    key_of = jax.random.split(jax.random.key(seed), 6)
    queries = draw_queries(jax.random.fold_in(key_of[5], 71), 0)
    key_rows = draw_key_rows(jax.random.fold_in(key_of[5], 71), 0)
    value_rows = scatter_about(key_of[2], (TOKENS, D), 1.0, 6.0, ((0, 32),))
    block_list = draw_block_list(jax.random.fold_in(key_of[5], 71), 0)
    block_count = draw_block_count(jax.random.fold_in(key_of[5], 71), 0)
    return dict(queries=queries, key_rows=key_rows, value_rows=value_rows, block_list=block_list, block_count=block_count)


def reference(queries, key_rows, value_rows, block_list, block_count):
    inv_root = 1.0 / (HEAD ** 0.5)
    query_tiles = queries.reshape(QTILES, BLOCK, HEADS, HEAD)
    key_blocks = key_rows.reshape(QTILES, BLOCK, HEADS, HEAD)
    value_blocks = value_rows.reshape(QTILES, BLOCK, HEADS, HEAD)

    def tile_attend(packed):
        query_tile, picked, live_count = packed
        key_sel = key_blocks[picked].reshape(LIST * BLOCK, HEADS, HEAD)
        value_sel = value_blocks[picked].reshape(LIST * BLOCK, HEADS, HEAD)
        scores = jnp.einsum("qhd,khd->hqk", query_tile.astype(jnp.float32), key_sel.astype(jnp.float32)) * inv_root
        live_keys = (jnp.arange(LIST * BLOCK, dtype=jnp.int32) // BLOCK) < live_count
        scores = jnp.where(live_keys[None, None, :], scores, -1e30)
        row_max = jnp.max(scores, axis=-1, keepdims=True)
        weights = jnp.where(live_keys[None, None, :], jnp.exp(scores - row_max), 0.0)
        row_sum = jnp.sum(weights, axis=-1)
        rounded = lax.optimization_barrier(weights.astype(jnp.bfloat16))
        mixed_out = jnp.einsum("hqk,khd->qhd", rounded.astype(jnp.float32), value_sel.astype(jnp.float32))
        return (mixed_out / jnp.transpose(row_sum)[:, :, None]).astype(jnp.bfloat16)

    result = lax.map(tile_attend, (query_tiles, block_list, block_count))
    return result.reshape(TOKENS, D)
```

```python
import functools
import math

import jax
import jax.numpy as jnp
from jax import lax
from jax.experimental import pallas as pl
from jax.experimental.pallas import tpu as pltpu
from jax.sharding import PartitionSpec as P

HEAD = 128
BLOCK = 128
LANES = 128
DEAD = -1e30
MESH = pl.DeviceIdType.MESH

TARGETS = {0: (1, 2, 3, 4), 1: (0, 2, 3, 5), 2: (3, 0, 1), 3: (2, 1, 7, 6)}


def head_groups(heads):
    quarter = max(1, heads // 4)
    groups = [(start, min(quarter, heads - start)) for start in range(0, heads, quarter)]
    parts, members = [], []
    for index, (start, count) in enumerate(groups):
        pieces = [(start, count)] if index < len(groups) - 1 else [(start + i, 1) for i in range(count)]
        members.append(list(range(len(parts), len(parts) + len(pieces))))
        parts += pieces
    return groups, parts, members


def stat_height(heads):
    return -(-2 * heads // 8) * 8


def is_folded(tm_count):
    return tm_count.bit_length() - 1 == 3


def kernel(
    tm_count, space_count, list_width,
    q_hbm, k_hbm, v_hbm, list_hbm, count_hbm, o_ref,
    list_ref, count_ref,
    q_own, k_own, v_own, k_halo, v_halo, k_band, v_band,
    top, total, mixed, near_bias, band_bias,
    local_sem, halo_send, halo_recv, band_send, band_recv,
    *guests,
):
    rows, width = q_hbm.shape
    blocks = rows // BLOCK
    picks = blocks // 2
    band_keys = picks * BLOCK
    heads = width // HEAD
    bits = tm_count.bit_length() - 1
    folded = is_folded(tm_count)
    groups, parts, members = head_groups(heads)
    all_parts = list(range(len(parts)))
    frame = lax.axis_index("tm")
    slab = lax.axis_index("space")
    scale = math.log2(math.e) / HEAD**0.5
    early = frame < tm_count // 2 if folded else frame >= 0
    place = jnp.where(early, frame, tm_count - 1 - frame)
    step = jnp.where(early, 1, -1)

    def flag(pred):
        return jnp.where(pred, 1, 0)

    def at(spot):
        return {"tm": jnp.where(early, spot, tm_count - 1 - spot)}

    def exists(delta):
        return (frame + delta >= 0) & (frame + delta < tm_count)

    def slab_exists(delta):
        return (slab + delta >= 0) & (slab + delta < space_count)

    def remote(src, dst, send_sem, recv_sem, device):
        return pltpu.make_async_remote_copy(
            src_ref=src, dst_ref=dst, send_sem=send_sem, recv_sem=recv_sem,
            device_id=device, device_id_type=MESH,
        )

    barrier = pltpu.get_barrier_semaphore()

    def greet(pred, device):
        @pl.when(pred)
        def _():
            pl.semaphore_signal(barrier, inc=1, device_id=device, device_id_type=MESH)

    expected = 0
    for delta in (-1, 1):
        expected = expected + flag(slab_exists(delta))
        greet(slab_exists(delta), {"space": slab + delta})
    if folded:
        last = tm_count - 1
        for role in TARGETS:
            expected = expected + jnp.where(place == role, len(TARGETS[role]), 0)
            for source, targets in TARGETS.items():
                if role in targets:
                    greet(place == role, at(source))
                if last - role in targets:
                    greet(place == role, at(last - source))
    else:
        for bit in range(bits):
            for delta in (1 << bit, -(1 << bit)):
                expected = expected + flag(exists(delta))
                greet(exists(delta), {"tm": frame + delta})
    pl.semaphore_wait(barrier, expected)

    def halo_copies(side, delta):
        start = (blocks - 1) * BLOCK if side == 0 else 0
        for index, (src, dst) in enumerate(((k_hbm, k_halo), (v_hbm, v_halo))):
            yield remote(
                src.at[pl.ds(start, BLOCK)], dst.at[side],
                halo_send.at[side, index], halo_recv.at[side, index],
                {"space": slab + delta},
            )

    def part_cols(part):
        start, count = parts[part]
        return pl.ds(start * HEAD, count * HEAD)

    def group_cols(group):
        start, count = groups[group]
        return pl.ds(start * HEAD, count * HEAD)

    def own_band(ref, parity):
        return ref.reshape(picks, 2, BLOCK, width).at[:, parity]

    def band_copies(channel, source, slot, part, device):
        kind, which = source
        for index, (own, band) in enumerate(((k_hbm, k_band), (v_hbm, v_band))):
            src = own_band(own, which) if kind == "own" else band.at[which]
            dst = band.at[slot]
            if part is not None:
                src = src.at[:, :, part_cols(part)]
                dst = dst.at[:, :, part_cols(part)]
            spot = 0 if part is None else part
            yield remote(
                src, dst, band_send.at[channel, spot, index], band_recv.at[slot, spot, index], device
            )

    def band_wait(slot, part):
        for copy in band_copies(0, ("band", slot), slot, part, {"tm": frame}):
            copy.wait_recv()

    local = [
        pltpu.make_async_copy(src, dst, local_sem.at[index])
        for index, (src, dst) in enumerate((
            (list_hbm, list_ref), (count_hbm, count_ref),
            (q_hbm, q_own), (k_hbm, k_own), (v_hbm, v_own),
        ))
    ]

    def start_halos():
        for side, delta in ((0, 1), (1, -1)):

            @pl.when(slab_exists(delta))
            def _(side=side, delta=delta):
                for copy in halo_copies(side, delta):
                    copy.start()

    frame_blocks = blocks * space_count
    first_block = frame * frame_blocks + slab * blocks

    def bias_rows(ids):
        row = jnp.concatenate([jnp.full((1, BLOCK), ident, jnp.int32) for ident in ids], axis=1)
        out = []
        for tile in range(blocks):
            count = count_ref[tile]
            value = jnp.full(row.shape, DEAD, jnp.float32)
            for entry in range(list_width):
                listed = jnp.where(entry < count, list_ref[tile, entry], -1)
                value = jnp.where(row == listed, 0.0, value)
            out.append(value)
        return out

    def fill_bias():
        for bit in range(bits):
            for side in (0, 1):
                partner = frame + (2 * side - 1) * step * (1 << bit)
                ids = [
                    partner * frame_blocks + slab * blocks + 2 * pick + bit % 2
                    for pick in range(picks)
                ]
                for tile, value in enumerate(bias_rows(ids)):
                    band_bias[2 * bit + side, tile : tile + 1, :] = value

    def fill_near():
        near_ids = [first_block + c for c in range(blocks)] + [first_block - 1, first_block + blocks]
        for tile, value in enumerate(bias_rows(near_ids)):
            near_bias[tile : tile + 1, :] = value

    def attend(get_k, get_v, get_bias, keys, mode="add", bounds=None, get_q=None, export=None):
        ones = jnp.ones((keys, HEAD), jnp.bfloat16)
        queries = get_q or (lambda cols: q_own[:, cols])

        def one_head(head, carry):
            cols = pl.ds(pl.multiple_of(head * HEAD, HEAD), HEAD)
            raw = lax.dot_general(
                queries(cols), get_k(cols), (((1,), (1,)), ((), ())),
                preferred_element_type=jnp.float32,
            )
            weights, shrink, tops = [], [], []
            for tile in range(blocks):
                span = slice(tile * BLOCK, (tile + 1) * BLOCK)
                scores = raw[span] * scale + get_bias(tile)
                peak = jnp.max(scores, axis=1, keepdims=True)
                if mode in ("first", "export"):
                    new_top = jnp.broadcast_to(peak, (BLOCK, HEAD))
                else:
                    old_top = top[head, span, :]
                    new_top = jnp.maximum(old_top, peak)
                    shrink.append(jnp.exp2(old_top - new_top))
                if mode in ("first", "add"):
                    top[head, span, :] = new_top
                tops.append(new_top)
                wide = jnp.concatenate([new_top] * (keys // HEAD), axis=1)
                weights.append(jnp.exp2(scores - wide).astype(jnp.bfloat16))
            extended = jnp.concatenate([get_v(cols), ones], axis=1)
            both = jnp.dot(
                jnp.concatenate(weights, axis=0), extended, preferred_element_type=jnp.float32
            )
            if mode == "export":
                export(head, cols, both[:, :HEAD], tops, both[:, HEAD:])
            elif mode == "first":
                mixed[head] = both[:, :HEAD]
                total[head] = both[:, HEAD:]
            else:
                factor = jnp.concatenate(shrink, axis=0)
                new_mixed = mixed[head] * factor + both[:, :HEAD]
                new_total = total[head] * factor + both[:, HEAD:]
                if mode == "final":
                    o_ref[:, cols] = (new_mixed / new_total).astype(o_ref.dtype)
                else:
                    mixed[head] = new_mixed
                    total[head] = new_total
            return carry

        start, count = (0, heads) if bounds is None else bounds
        paired = count - count % 2
        if paired > 2:
            lax.fori_loop(start, start + paired, one_head, 0, unroll=2)
        for head in range(start if paired <= 2 else start + paired, start + count):
            one_head(head, 0)

    def attend_own():
        attend(
            lambda cols: k_own[:, cols],
            lambda cols: v_own[:, cols],
            lambda tile: near_bias[tile : tile + 1, : blocks * BLOCK],
            blocks * BLOCK,
            mode="first",
        )

    def attend_halos():
        for side, delta in ((0, -1), (1, 1)):

            @pl.when(slab_exists(delta))
            def _(side=side, delta=delta):
                for copy in halo_copies(side, delta):
                    copy.wait_recv()
                start = (blocks + side) * BLOCK
                attend(
                    lambda cols: k_halo[side, :, cols],
                    lambda cols: v_halo[side, :, cols],
                    lambda tile: near_bias[tile : tile + 1, start : start + BLOCK],
                    BLOCK,
                )

    def in_slot(slot):
        return (
            lambda cols: k_band[slot, :, :, cols].reshape(band_keys, HEAD),
            lambda cols: v_band[slot, :, :, cols].reshape(band_keys, HEAD),
            lambda tile: band_bias[slot, tile : tile + 1, :],
        )

    def joined(sources):
        def join(index, axis):
            return lambda arg: jnp.concatenate([s[index](arg) for s in sources], axis=axis)

        return join(0, 0), join(1, 0), join(2, 1)

    if not folded:
        start_halos()
        for bit in list(range(1, bits)) + [0]:
            for side, delta in ((0, 1 << bit), (1, -(1 << bit))):

                @pl.when(exists(delta))
                def _(bit=bit, side=side, delta=delta):
                    slot = 2 * bit + side
                    for copy in band_copies(slot, ("own", bit % 2), slot, None, {"tm": frame + delta}):
                        copy.start()

        for copy in local:
            copy.start()
        for copy in local[:2]:
            copy.wait()
        fill_near()
        fill_bias()
        for copy in local[2:]:
            copy.wait()
        attend_own()
        attend_halos()
        for bit in list(range(1, bits)) + [0]:
            for side, delta in ((0, -(1 << bit)), (1, 1 << bit)):

                @pl.when(exists(delta))
                def _(bit=bit, side=side):
                    slot = 2 * bit + side
                    band_wait(slot, None)
                    attend(*in_slot(slot), band_keys)

        def finish(head, carry):
            cols = pl.ds(pl.multiple_of(head * HEAD, HEAD), HEAD)
            o_ref[:, cols] = (mixed[head] / total[head]).astype(o_ref.dtype)
            return carry

        lax.fori_loop(0, heads, finish, 0)
        for bit in range(bits):
            for side, delta in ((0, 1 << bit), (1, -(1 << bit))):

                @pl.when(exists(delta))
                def _(bit=bit, side=side, delta=delta):
                    slot = 2 * bit + side
                    for copy in band_copies(slot, ("own", bit % 2), slot, None, {"tm": frame + delta}):
                        copy.wait_send()

    else:
        (
            guest, away, guest_bias, stat_rows, stat_out, stat_in,
            guest_send, guest_recv, bias_send, bias_recv, stat_send, stat_recv,
        ) = guests
        upper = len(groups) // 2
        low_groups, high_groups = range(upper), range(upper, len(groups))
        low_parts = [part for group in low_groups for part in members[group]]
        low_span = (0, groups[upper][0])
        every, high = range(len(groups)), high_groups

        channels = {
            0: [
                (("own", 0), 1, 0, [None]),
                (("own", 1), 2, 2, low_parts),
                (("band", 5), 3, 1, all_parts),
            ],
            1: [
                (("own", 0), 0, 1, [None]),
                (("own", 0), 2, 0, low_parts),
                (("own", 1), 3, 2, all_parts),
                (("own", 0), 5, 5, all_parts),
                (("band", 3), 5, 3, all_parts),
            ],
            2: [
                (("own", 0), 3, 0, [None]),
                (("own", 1), 0, 3, all_parts),
                (("own", 0), 1, 1, all_parts),
            ],
            3: [
                (("own", 0), 2, 1, [None]),
                (("own", 1), 1, 3, all_parts),
                (("own", 0), 7, 5, all_parts),
                (("band", 0), 6, 5, all_parts),
            ],
        }

        def channel_copies(role, index, only=None):
            source, target, slot, some = channels[role][index]
            for part in some:
                if only is None or part in only:
                    yield from band_copies(index, source, slot, part, at(target))

        def start_channel(role, index, only=None):
            for copy in channel_copies(role, index, only):
                copy.start()

        guest_groups = (every, high)
        guest_host = (7, 0)
        guest_home = (4, 2)
        guest_slots = ((5, 3), (2, 0))

        def query_copy(index, group):
            cols = group_cols(group)
            return remote(
                q_hbm.at[:, cols], guest.at[index, :, cols],
                guest_send.at[index, group], guest_recv.at[index, group], at(guest_host[index]),
            )

        def bias_copy(index, which):
            return remote(
                band_bias.at[guest_slots[index][which]], guest_bias.at[2 * index + which],
                bias_send.at[which], bias_recv.at[2 * index + which], at(guest_host[index]),
            )

        def result_copy(index, group):
            cols = group_cols(group)
            return remote(
                away.at[index, :, cols], guest.at[0, :, cols],
                guest_send.at[index, group], guest_recv.at[0, group], at(guest_home[index]),
            )

        def stat_copy(index):
            return remote(
                stat_out.at[index], stat_in, stat_send.at[index], stat_recv.at[0], at(guest_home[index])
            )

        def guest_base(index):
            return groups[guest_groups[index][0]][0]

        def host(index, group, sources):
            base = guest_base(index)
            lane = lax.broadcasted_iota(jnp.int32, (BLOCK, LANES), 1)

            def export(head, cols, value, tops, sums):
                away[index, :, cols] = value.astype(away.dtype)
                for tile in range(blocks):
                    span = slice(tile * BLOCK, (tile + 1) * BLOCK)
                    held = jnp.where(lane == head - base, tops[tile], stat_rows[tile])
                    stat_rows[tile] = jnp.where(lane == heads + head - base, sums[span], held)

            attend(
                *joined(sources), 2 * band_keys, mode="export", bounds=groups[group],
                get_q=lambda cols: guest[index, :, cols], export=export,
            )
            result_copy(index, group).start()

        def host_source(index, which, parity=None, slot=None):
            def bias(tile):
                return guest_bias[2 * index + which, tile : tile + 1, :]

            if slot is not None:
                get_k, get_v, _ = in_slot(slot)
                return get_k, get_v, bias

            def own(ref):
                return lambda cols: jnp.concatenate(
                    [ref[pl.ds((2 * pick + parity) * BLOCK, BLOCK), cols] for pick in range(picks)], axis=0
                )

            return own(k_own), own(v_own), bias

        def send_stats(index):
            height = stat_out.shape[2]
            for tile in range(blocks):
                stat_out[index, tile] = jnp.transpose(stat_rows[tile])[:height]
            stat_copy(index).start()

        def merge(index):
            base = guest_base(index)
            for group in guest_groups[index]:
                result_copy(index, group).wait_recv()
            stat_copy(index).wait_recv()
            height = stat_in.shape[1]
            for tile in range(blocks):
                packed = jnp.concatenate(
                    [stat_in[tile], jnp.zeros((LANES - height, BLOCK), jnp.float32)], axis=0
                )
                stat_rows[tile] = jnp.transpose(packed)

            def one_tile(tile, carry):
                span = pl.ds(pl.multiple_of(tile * BLOCK, BLOCK), BLOCK)
                for head in range(base, heads):
                    cols = pl.ds(head * HEAD, HEAD)
                    held = stat_rows[tile]
                    their_top = jnp.broadcast_to(held[:, head - base : head - base + 1], (BLOCK, HEAD))
                    spot = heads + head - base
                    their_sum = jnp.broadcast_to(held[:, spot : spot + 1], (BLOCK, HEAD))
                    old_top = top[head, span, :]
                    new_top = jnp.maximum(old_top, their_top)
                    ours, theirs = jnp.exp2(old_top - new_top), jnp.exp2(their_top - new_top)
                    value = guest[0, span, cols].astype(jnp.float32)
                    top[head, span, :] = new_top
                    mixed[head, span, :] = mixed[head, span, :] * ours + value * theirs
                    total[head, span, :] = total[head, span, :] * ours + their_sum * theirs
                return carry

            lax.fori_loop(0, blocks, one_tile, 0)

        is_place = [place == role for role in range(4)]

        @pl.when(is_place[3])
        def _():
            for group in every:
                query_copy(0, group).start()

        @pl.when(is_place[2])
        def _():
            for group in high:
                query_copy(1, group).start()

        for role, firsts in ((0, (0, 1)), (1, (0, 1, 2, 3)), (2, (0,)), (3, (0, 1))):

            @pl.when(is_place[role])
            def _(role=role, firsts=firsts):
                for index in firsts:
                    start_channel(role, index)

        start_halos()
        for copy in local:
            copy.start()
        for copy in local[:2]:
            copy.wait()
        fill_bias()
        for role, index, rest in ((2, 1, (1, 2)), (3, 0, (2,))):

            @pl.when(is_place[role])
            def _(role=role, index=index, rest=rest):
                for which in (0, 1):
                    bias_copy(index, which).start()
                for channel in rest:
                    start_channel(role, channel)

        fill_near()

        @pl.when(is_place[0])
        def _():
            stat_rows[...] = jnp.zeros_like(stat_rows)

        for copy in local[2:]:
            copy.wait()
        attend_own()

        beside = 1 - lax.rem(place, 2)
        band_wait(beside, None)

        @pl.when(is_place[3])
        def _():
            start_channel(3, 3)

        def relay(role, channel, slot, some):
            for part in some:
                band_wait(slot, part)
                start_channel(role, channel, [part])

        @pl.when(is_place[1])
        def _():
            relay(1, 4, 3, members[0])

        attend(*in_slot(beside), band_keys)
        attend_halos()

        @pl.when(is_place[0])
        def _():
            for index in (1, 0):
                for which in (0, 1):
                    bias_copy(index, which).wait_recv()
            for group in high:
                query_copy(1, group).wait_recv()
                host(1, group, [host_source(1, 0, parity=1), host_source(1, 1, slot=1)])
            send_stats(1)
            for group in every:
                relay(0, 2, 5, members[group])
                query_copy(0, group).wait_recv()
                for part in members[group]:
                    band_wait(3, part)
                host(0, group, [host_source(0, 0, parity=0), host_source(0, 1, slot=3)])
            send_stats(0)

        @pl.when(is_place[1])
        def _():
            for group in every[1:]:
                relay(1, 4, 3, members[group])
            attend(*in_slot(3), band_keys)

        @pl.when(is_place[2])
        def _():
            for part in low_parts:
                band_wait(2, part)
                band_wait(0, part)
            attend(*joined([in_slot(2), in_slot(0)]), 2 * band_keys, bounds=low_span)
            merge(1)

        @pl.when(is_place[3])
        def _():
            merge(0)

        early_slot = jnp.where(place == 3, 2, 5)
        late_slot = jnp.where(lax.rem(place, 2) == 0, 3, 1)
        for part in all_parts:

            @pl.when(jnp.logical_not(is_place[0]))
            def _(part=part):
                band_wait(early_slot, part)
                band_wait(late_slot, part)

            attend(
                *joined([in_slot(early_slot), in_slot(late_slot)]), 2 * band_keys,
                mode="final", bounds=parts[part],
            )

        for role in channels:

            @pl.when(is_place[role])
            def _(role=role):
                for index in range(len(channels[role])):
                    for copy in channel_copies(role, index):
                        copy.wait_send()
                for index, home in ((0, 3), (1, 2)):
                    if role == home:
                        for group in guest_groups[index]:
                            query_copy(index, group).wait_send()
                        for which in (0, 1):
                            bias_copy(index, which).wait_send()
                    if role == 0:
                        for group in guest_groups[index]:
                            result_copy(index, group).wait_send()
                        stat_copy(index).wait_send()

    for side, delta in ((0, 1), (1, -1)):

        @pl.when(slab_exists(delta))
        def _(side=side, delta=delta):
            for copy in halo_copies(side, delta):
                copy.wait_send()


def shards(tm_count, space_count, queries, key_rows, value_rows, block_list, block_count):
    rows, width = queries.shape
    blocks = rows // BLOCK
    picks = blocks // 2
    heads = width // HEAD
    slots = 2 * (tm_count.bit_length() - 1)
    kind = key_rows.dtype
    groups, parts, _ = head_groups(heads)
    in_hbm = pl.BlockSpec(memory_space=pltpu.HBM)
    dma = pltpu.SemaphoreType.DMA
    scratch = [
        pltpu.SMEM(block_list.shape, block_list.dtype),
        pltpu.SMEM(block_count.shape, block_count.dtype),
        pltpu.VMEM((rows, width), kind),
        pltpu.VMEM((rows, width), kind),
        pltpu.VMEM((rows, width), kind),
        pltpu.VMEM((2, BLOCK, width), kind),
        pltpu.VMEM((2, BLOCK, width), kind),
        pltpu.VMEM((slots, picks, BLOCK, width), kind),
        pltpu.VMEM((slots, picks, BLOCK, width), kind),
        pltpu.VMEM((heads, rows, HEAD), jnp.float32),
        pltpu.VMEM((heads, rows, HEAD), jnp.float32),
        pltpu.VMEM((heads, rows, HEAD), jnp.float32),
        pltpu.VMEM((blocks, (blocks + 2) * BLOCK), jnp.float32),
        pltpu.VMEM((slots, blocks, picks * BLOCK), jnp.float32),
        dma((5,)),
        dma((2, 2)),
        dma((2, 2)),
        dma((slots, len(parts), 2)),
        dma((slots, len(parts), 2)),
    ]
    if is_folded(tm_count):
        height = stat_height(heads)
        scratch += [
            pltpu.VMEM((2, rows, width), kind),
            pltpu.VMEM((2, rows, width), kind),
            pltpu.VMEM((4, blocks, picks * BLOCK), jnp.float32),
            pltpu.VMEM((blocks, BLOCK, LANES), jnp.float32),
            pltpu.VMEM((2, blocks, height, BLOCK), jnp.float32),
            pltpu.VMEM((blocks, height, BLOCK), jnp.float32),
            dma((2, len(groups))),
            dma((2, len(groups))),
            dma((2,)),
            dma((4,)),
            dma((2,)),
            dma((1,)),
        ]
    return pl.pallas_call(
        functools.partial(kernel, tm_count, space_count, block_list.shape[1]),
        out_shape=jax.ShapeDtypeStruct((rows, width), queries.dtype),
        in_specs=[in_hbm] * 5,
        out_specs=pl.BlockSpec(memory_space=pltpu.VMEM),
        scratch_shapes=scratch,
        compiler_params=pltpu.CompilerParams(
            collective_id=0, has_side_effects=True, vmem_limit_bytes=50 * 1024 * 1024
        ),
    )(*[
        pltpu.with_memory_space_constraint(array, pltpu.HBM)
        for array in (queries, key_rows, value_rows, block_list, block_count)
    ])


def solution(mesh):
    placed = (
        P(("tm", "space"), None),
        P(("tm", "space"), None),
        P(("tm", "space"), None),
        P(("tm", "space"), None),
        P(("tm", "space")),
    )
    return jax.shard_map(
        functools.partial(shards, mesh.shape["tm"], mesh.shape["space"]),
        mesh=mesh, in_specs=placed, out_specs=P(("tm", "space"), None), check_vma=False,
    )
```

```python
import functools
import math

import jax
import jax.numpy as jnp
from jax import lax
from jax.experimental import pallas as pl
from jax.experimental.pallas import tpu as pltpu
from jax.sharding import PartitionSpec as P

HEAD = 128
BLOCK = 128
LANES = 128
DEAD = -1e30
MESH = pl.DeviceIdType.MESH

TARGETS = {0: (1, 2, 3, 4), 1: (0, 2, 3, 5), 2: (3, 0, 1), 3: (2, 1, 7, 6)}


def head_groups(heads):
    quarter = max(1, heads // 4)
    groups = [(start, min(quarter, heads - start)) for start in range(0, heads, quarter)]
    parts, members = [], []
    for index, (start, count) in enumerate(groups):
        pieces = [(start, count)] if index < len(groups) - 1 else [(start + i, 1) for i in range(count)]
        members.append(list(range(len(parts), len(parts) + len(pieces))))
        parts += pieces
    return groups, parts, members


def stat_height(heads):
    return -(-2 * max(count for _, count in head_groups(heads)[0]) // 8) * 8


def is_folded(tm_count):
    return tm_count.bit_length() - 1 == 3


def kernel(
    tm_count, space_count, list_width,
    q_hbm, k_hbm, v_hbm, list_hbm, count_hbm, o_ref,
    list_ref, count_ref,
    q_own, k_own, v_own, k_halo, v_halo, k_band, v_band,
    top, total, mixed, near_bias, band_bias,
    local_sem, halo_send, halo_recv, band_send, band_recv,
    *guests,
):
    rows, width = q_hbm.shape
    blocks = rows // BLOCK
    picks = blocks // 2
    band_keys = picks * BLOCK
    heads = width // HEAD
    bits = tm_count.bit_length() - 1
    folded = is_folded(tm_count)
    groups, parts, members = head_groups(heads)
    all_parts = list(range(len(parts)))
    frame = lax.axis_index("tm")
    slab = lax.axis_index("space")
    scale = math.log2(math.e) / HEAD**0.5
    early = frame < tm_count // 2 if folded else frame >= 0
    place = jnp.where(early, frame, tm_count - 1 - frame)
    step = jnp.where(early, 1, -1)

    def flag(pred):
        return jnp.where(pred, 1, 0)

    def at(spot):
        return {"tm": jnp.where(early, spot, tm_count - 1 - spot)}

    def exists(delta):
        return (frame + delta >= 0) & (frame + delta < tm_count)

    def slab_exists(delta):
        return (slab + delta >= 0) & (slab + delta < space_count)

    def remote(src, dst, send_sem, recv_sem, device):
        return pltpu.make_async_remote_copy(
            src_ref=src, dst_ref=dst, send_sem=send_sem, recv_sem=recv_sem,
            device_id=device, device_id_type=MESH,
        )

    barrier = pltpu.get_barrier_semaphore()

    def greet(pred, device):
        @pl.when(pred)
        def _():
            pl.semaphore_signal(barrier, inc=1, device_id=device, device_id_type=MESH)

    expected = 0
    for delta in (-1, 1):
        expected = expected + flag(slab_exists(delta))
        greet(slab_exists(delta), {"space": slab + delta})
    if folded:
        last = tm_count - 1
        for role in TARGETS:
            expected = expected + jnp.where(place == role, len(TARGETS[role]), 0)
            for source, targets in TARGETS.items():
                if role in targets:
                    greet(place == role, at(source))
                if last - role in targets:
                    greet(place == role, at(last - source))
    else:
        for bit in range(bits):
            for delta in (1 << bit, -(1 << bit)):
                expected = expected + flag(exists(delta))
                greet(exists(delta), {"tm": frame + delta})
    def halo_copies(side, delta):
        start = (blocks - 1) * BLOCK if side == 0 else 0
        for src, dst in ((k_hbm, k_halo), (v_hbm, v_halo)):
            yield remote(
                src.at[pl.ds(start, BLOCK)], dst.at[side],
                halo_send.at[side], halo_recv.at[side], {"space": slab + delta},
            )

    def halo_wait(side, delta):
        return remote(k_halo, k_halo, halo_send.at[side], halo_recv.at[side], {"space": slab + delta})

    def columns(start, count):
        return pl.ds(start * HEAD, count * HEAD)

    whole = [(0, 0, heads)]
    group_pieces = [(members[i][0], *group) for i, group in enumerate(groups)]
    part_pieces = [(i, *part) for i, part in enumerate(parts)]

    def own_band(ref, parity):
        return ref.reshape(picks, 2, BLOCK, width).at[:, parity]

    def band_copies(channel, source, slot, pieces, device):
        kind, which = source
        for spot, start, count in pieces:
            cols = columns(start, count)
            for own, band in ((k_hbm, k_band), (v_hbm, v_band)):
                src = own_band(own, which) if kind == "own" else band.at[which]
                yield remote(
                    src.at[:, :, cols], band.at[slot].at[:, :, cols],
                    band_send.at[channel], band_recv.at[slot, spot], device,
                )

    def band_bytes(channel, slot, spot, count):
        both = k_band.at[pl.ds(0, 2), :, :, columns(0, count)]
        return remote(both, both, band_send.at[channel], band_recv.at[slot, spot], {"tm": frame})

    def band_wait(slot, piece):
        band_bytes(0, slot, piece[0], piece[2]).wait_recv()

    def sent_wait(channel, pieces):
        band_bytes(channel, 0, 0, sum(piece[2] for piece in pieces)).wait_send()

    local = [
        pltpu.make_async_copy(src, dst, local_sem.at[index])
        for index, (src, dst) in enumerate((
            (list_hbm, list_ref), (count_hbm, count_ref),
            (q_hbm, q_own), (k_hbm, k_own), (v_hbm, v_own),
        ))
    ]
    for copy in local:
        copy.start()

    def start_halos():
        for side, delta in ((0, 1), (1, -1)):

            @pl.when(slab_exists(delta))
            def _(side=side, delta=delta):
                for copy in halo_copies(side, delta):
                    copy.start()

    def halos_sent():
        for side, delta in ((0, 1), (1, -1)):

            @pl.when(slab_exists(delta))
            def _(side=side, delta=delta):
                halo_wait(side, delta).wait_send()

    frame_blocks = blocks * space_count
    first_block = frame * frame_blocks + slab * blocks

    def bias_rows(ids):
        row = jnp.concatenate([jnp.full((1, BLOCK), ident, jnp.int32) for ident in ids], axis=1)
        out = []
        for tile in range(blocks):
            count = count_ref[tile]
            value = jnp.full(row.shape, DEAD, jnp.float32)
            for entry in range(list_width):
                listed = jnp.where(entry < count, list_ref[tile, entry], -1)
                value = jnp.where(row == listed, 0.0, value)
            out.append(value)
        return out

    def fill_bias():
        for bit in range(bits):
            for side in (0, 1):
                partner = frame + (2 * side - 1) * step * (1 << bit)
                ids = [
                    partner * frame_blocks + slab * blocks + 2 * pick + bit % 2
                    for pick in range(picks)
                ]
                for tile, value in enumerate(bias_rows(ids)):
                    band_bias[2 * bit + side, tile : tile + 1, :] = value

    def fill_near():
        near_ids = [first_block + c for c in range(blocks)] + [first_block - 1, first_block + blocks]
        for tile, value in enumerate(bias_rows(near_ids)):
            near_bias[tile : tile + 1, :] = value

    def attend(get_k, get_v, get_bias, keys, mode="add", bounds=None, get_q=None, export=None):
        ones = jnp.ones((keys, HEAD), jnp.bfloat16)
        queries = get_q or (lambda cols: q_own[:, cols])

        def one_head(head, carry):
            cols = pl.ds(pl.multiple_of(head * HEAD, HEAD), HEAD)
            raw = lax.dot_general(
                queries(cols), get_k(cols), (((1,), (1,)), ((), ())),
                preferred_element_type=jnp.float32,
            )
            weights, shrink, tops = [], [], []
            for tile in range(blocks):
                span = slice(tile * BLOCK, (tile + 1) * BLOCK)
                scores = raw[span] * scale + get_bias(tile)
                peak = jnp.max(scores, axis=1, keepdims=True)
                if mode in ("first", "export"):
                    new_top = jnp.broadcast_to(peak, (BLOCK, HEAD))
                else:
                    old_top = top[head, span, :]
                    new_top = jnp.maximum(old_top, peak)
                    shrink.append(jnp.exp2(old_top - new_top))
                if mode in ("first", "add"):
                    top[head, span, :] = new_top
                tops.append(new_top)
                wide = jnp.concatenate([new_top] * (keys // HEAD), axis=1)
                weights.append(jnp.exp2(scores - wide).astype(jnp.bfloat16))
            extended = jnp.concatenate([get_v(cols), ones], axis=1)
            both = jnp.dot(
                jnp.concatenate(weights, axis=0), extended, preferred_element_type=jnp.float32
            )
            if mode == "export":
                export(head, cols, both[:, :HEAD], tops, both[:, HEAD:])
            elif mode == "first":
                mixed[head] = both[:, :HEAD]
                total[head] = both[:, HEAD:]
            else:
                factor = jnp.concatenate(shrink, axis=0)
                new_mixed = mixed[head] * factor + both[:, :HEAD]
                new_total = total[head] * factor + both[:, HEAD:]
                if mode == "final":
                    o_ref[:, cols] = (new_mixed / new_total).astype(o_ref.dtype)
                else:
                    mixed[head] = new_mixed
                    total[head] = new_total
            return carry

        start, count = (0, heads) if bounds is None else bounds
        paired = count - count % 2
        if export is not None:
            paired = 0
        if paired > 2:
            lax.fori_loop(start, start + paired, one_head, 0, unroll=2)
        for head in range(start if paired <= 2 else start + paired, start + count):
            one_head(head, 0)

    def attend_own():
        attend(
            lambda cols: k_own[:, cols],
            lambda cols: v_own[:, cols],
            lambda tile: near_bias[tile : tile + 1, : blocks * BLOCK],
            blocks * BLOCK,
            mode="first",
        )

    def attend_halos():
        for side, delta in ((0, -1), (1, 1)):

            @pl.when(slab_exists(delta))
            def _(side=side, delta=delta):
                halo_wait(side, delta).wait_recv()
                start = (blocks + side) * BLOCK
                attend(
                    lambda cols: k_halo[side, :, cols],
                    lambda cols: v_halo[side, :, cols],
                    lambda tile: near_bias[tile : tile + 1, start : start + BLOCK],
                    BLOCK,
                )

    def in_slot(slot):
        return (
            lambda cols: k_band[slot, :, :, cols].reshape(band_keys, HEAD),
            lambda cols: v_band[slot, :, :, cols].reshape(band_keys, HEAD),
            lambda tile: band_bias[slot, tile : tile + 1, :],
        )

    def joined(sources):
        def join(index, axis):
            return lambda arg: jnp.concatenate([s[index](arg) for s in sources], axis=axis)

        return join(0, 0), join(1, 0), join(2, 1)

    for copy in local[:2]:
        copy.wait()
    fill_bias()
    fill_near()
    pl.semaphore_wait(barrier, expected)

    if not folded:
        start_halos()
        for bit in list(range(1, bits)) + [0]:
            for side, delta in ((0, 1 << bit), (1, -(1 << bit))):

                @pl.when(exists(delta))
                def _(bit=bit, side=side, delta=delta):
                    slot = 2 * bit + side
                    for copy in band_copies(slot, ("own", bit % 2), slot, whole, {"tm": frame + delta}):
                        copy.start()

        for copy in local[2:]:
            copy.wait()
        attend_own()
        attend_halos()
        for bit in list(range(1, bits)) + [0]:
            for side, delta in ((0, -(1 << bit)), (1, 1 << bit)):

                @pl.when(exists(delta))
                def _(bit=bit, side=side):
                    slot = 2 * bit + side
                    band_wait(slot, whole[0])
                    attend(*in_slot(slot), band_keys)

        def finish(head, carry):
            cols = pl.ds(pl.multiple_of(head * HEAD, HEAD), HEAD)
            o_ref[:, cols] = (mixed[head] / total[head]).astype(o_ref.dtype)
            return carry

        lax.fori_loop(0, heads, finish, 0)
        for bit in range(bits):
            for side, delta in ((0, 1 << bit), (1, -(1 << bit))):

                @pl.when(exists(delta))
                def _(slot=2 * bit + side):
                    sent_wait(slot, whole)

        halos_sent()

    else:
        (
            guest, away, guest_bias, stat_out, stat_in,
            guest_send, guest_recv, bias_send, bias_recv, stat_send, stat_recv,
        ) = guests
        upper = len(groups) // 2
        every, high = range(len(groups)), range(upper, len(groups))
        low_pieces = group_pieces[:upper]
        low_span = (0, groups[upper][0])

        channels = {
            0: [
                (("own", 0), 1, 0, whole),
                (("own", 1), 2, 2, low_pieces),
                (("band", 5), 3, 1, part_pieces),
            ],
            1: [
                (("own", 0), 0, 1, whole),
                (("own", 0), 2, 0, low_pieces),
                (("own", 1), 3, 2, group_pieces),
                (("own", 0), 5, 5, group_pieces),
                (("band", 3), 5, 3, part_pieces),
            ],
            2: [
                (("own", 0), 3, 0, whole),
                (("own", 1), 0, 3, group_pieces),
                (("own", 0), 1, 1, part_pieces),
            ],
            3: [
                (("own", 0), 2, 1, whole),
                (("own", 1), 1, 3, group_pieces),
                (("own", 0), 7, 5, group_pieces),
                (("band", 0), 6, 5, group_pieces),
            ],
        }

        def start_channel(role, index, spots=None):
            source, target, slot, pieces = channels[role][index]
            pieces = [piece for piece in pieces if spots is None or piece[0] in spots]
            for copy in band_copies(index, source, slot, pieces, at(target)):
                copy.start()

        def channels_sent(role, *indices):
            for index in indices:
                sent_wait(index, channels[role][index][3])

        guest_groups = (every, high)
        guest_host = (7, 0)
        guest_home = (4, 2)
        guest_slots = ((5, 3), (2, 0))

        def query_copy(index, group):
            cols = columns(*groups[group])
            return remote(
                q_hbm.at[:, cols], guest.at[index, :, cols],
                guest_send.at[index], guest_recv.at[index, group], at(guest_host[index]),
            )

        def guest_sent(index):
            cols = columns(0, sum(groups[group][1] for group in guest_groups[index]))
            ref = guest.at[index, :, cols]
            remote(ref, ref, guest_send.at[index], guest_recv.at[index, 0], {"tm": frame}).wait_send()

        def bias_copy(index, which):
            return remote(
                band_bias.at[guest_slots[index][which]], guest_bias.at[2 * index + which],
                bias_send.at[0], bias_recv.at[index], at(guest_host[index]),
            )

        def bias_wait(index):
            pair = guest_bias.at[pl.ds(2 * index, 2)]
            return remote(pair, pair, bias_send.at[0], bias_recv.at[index], {"tm": frame})

        def result_copy(index, group):
            cols = columns(*groups[group])
            return remote(
                away.at[index, :, cols], guest.at[0, :, cols],
                guest_send.at[index], guest_recv.at[0, group], at(guest_home[index]),
            )

        def stat_copy(index, group):
            return remote(
                stat_out.at[index, group], stat_in.at[group],
                stat_send.at[index], stat_recv.at[group], at(guest_home[index]),
            )

        def stat_sent(index):
            ref = stat_out.at[index, pl.ds(0, len(guest_groups[index]))]
            remote(ref, ref, stat_send.at[index], stat_recv.at[0], {"tm": frame}).wait_send()

        height = stat_height(heads)

        def host(index, group, sources):
            held = []

            def export(head, cols, value, tops, sums):
                away[index, :, cols] = value.astype(away.dtype)
                held.append((tops, sums))

            attend(
                *joined(sources), 2 * band_keys, mode="export", bounds=groups[group],
                get_q=lambda cols: guest[index, :, cols], export=export,
            )
            result_copy(index, group).start()
            lane = lax.broadcasted_iota(jnp.int32, (BLOCK, LANES), 1)
            for tile in range(blocks):
                packed = jnp.zeros((BLOCK, LANES), jnp.float32)
                for place_in, (tops, sums) in enumerate(held):
                    span = slice(tile * BLOCK, (tile + 1) * BLOCK)
                    packed = jnp.where(lane == 2 * place_in, tops[tile], packed)
                    packed = jnp.where(lane == 2 * place_in + 1, sums[span], packed)
                stat_out[index, group, tile] = jnp.transpose(packed)[:height]
            stat_copy(index, group).start()

        def host_source(index, which, parity=None, slot=None):
            def bias(tile):
                return guest_bias[2 * index + which, tile : tile + 1, :]

            if slot is not None:
                get_k, get_v, _ = in_slot(slot)
                return get_k, get_v, bias

            def own(ref):
                return lambda cols: jnp.concatenate(
                    [ref[pl.ds((2 * pick + parity) * BLOCK, BLOCK), cols] for pick in range(picks)], axis=0
                )

            return own(k_own), own(v_own), bias

        def merge(group):
            start, count = groups[group]
            result_copy(0, group).wait_recv()
            stat_copy(0, group).wait_recv()

            def one_tile(tile, carry):
                span = pl.ds(pl.multiple_of(tile * BLOCK, BLOCK), BLOCK)
                packed = jnp.concatenate(
                    [stat_in[group, tile], jnp.zeros((LANES - height, BLOCK), jnp.float32)], axis=0
                )
                stats = jnp.transpose(packed)
                for index in range(count):
                    head = start + index
                    their_top = jnp.broadcast_to(stats[:, 2 * index : 2 * index + 1], (BLOCK, HEAD))
                    their_sum = jnp.broadcast_to(stats[:, 2 * index + 1 : 2 * index + 2], (BLOCK, HEAD))
                    old_top = top[head, span, :]
                    new_top = jnp.maximum(old_top, their_top)
                    ours, theirs = jnp.exp2(old_top - new_top), jnp.exp2(their_top - new_top)
                    value = guest[0, span, columns(head, 1)].astype(jnp.float32)
                    top[head, span, :] = new_top
                    mixed[head, span, :] = mixed[head, span, :] * ours + value * theirs
                    total[head, span, :] = total[head, span, :] * ours + their_sum * theirs
                return carry

            lax.fori_loop(0, blocks, one_tile, 0)

        is_place = [place == role for role in range(4)]

        @pl.when(is_place[0])
        def _():
            start_channel(0, 1)
            start_channel(0, 0)

        @pl.when(is_place[1])
        def _():
            for index in (1, 3, 0, 2):
                start_channel(1, index)

        @pl.when(is_place[2])
        def _():
            for group in high:
                query_copy(1, group).start()
            for which in (0, 1):
                bias_copy(1, which).start()
            start_channel(2, 0)
            start_channel(2, 1)

        @pl.when(is_place[3])
        def _():
            start_channel(3, 1)
            for group in every:
                query_copy(0, group).start()
            for which in (0, 1):
                bias_copy(0, which).start()
            start_channel(3, 0)

        start_halos()

        @pl.when(is_place[2])
        def _():
            start_channel(2, 2)

        @pl.when(is_place[3])
        def _():
            start_channel(3, 2)

        for copy in local[2:]:
            copy.wait()
        attend_own()

        beside = 1 - lax.rem(place, 2)
        band_wait(beside, whole[0])

        @pl.when(is_place[3])
        def _():
            start_channel(3, 3)

        def relay(role, channel, slot, group):
            band_wait(slot, group_pieces[group])
            start_channel(role, channel, members[group])

        @pl.when(is_place[1])
        def _():
            relay(1, 4, 3, 0)

        attend(*in_slot(beside), band_keys)

        @pl.when(is_place[0])
        def _():
            bias_wait(1).wait_recv()
            for group in high:
                query_copy(1, group).wait_recv()
                host(1, group, [host_source(1, 0, parity=1), host_source(1, 1, slot=1)])

        @pl.when(is_place[1])
        def _():
            relay(1, 4, 3, 1)

        attend_halos()

        @pl.when(is_place[0])
        def _():
            bias_wait(0).wait_recv()
            for group in every:
                relay(0, 2, 5, group)
                query_copy(0, group).wait_recv()
                band_wait(3, group_pieces[group])
                host(0, group, [host_source(0, 0, parity=0), host_source(0, 1, slot=3)])
            channels_sent(0, 0, 1)
            guest_sent(1)
            stat_sent(1)

        @pl.when(is_place[1])
        def _():
            for group in every[2:]:
                relay(1, 4, 3, group)
            attend(*in_slot(3), band_keys)
            channels_sent(1, 0, 1, 3)

        @pl.when(is_place[2])
        def _():
            for piece in low_pieces:
                band_wait(2, piece)
                band_wait(0, piece)
            attend(*joined([in_slot(2), in_slot(0)]), 2 * band_keys, bounds=low_span)
            guest_sent(1)
            bias_wait(1).wait_send()
            channels_sent(2, 0)

        @pl.when(is_place[3])
        def _():
            guest_sent(0)
            bias_wait(0).wait_send()
            channels_sent(3, 0, 1)

        halos_sent()
        early_slot = jnp.where(is_place[3], 2, 5)
        late_slot = jnp.where(lax.rem(place, 2) == 0, 3, 1)
        for group in every:
            if group == len(groups) - 1:

                @pl.when(is_place[0])
                def _():
                    guest_sent(0)
                    stat_sent(0)

                @pl.when(is_place[1])
                def _():
                    channels_sent(1, 4)

                @pl.when(is_place[2])
                def _():
                    channels_sent(2, 1)

                @pl.when(is_place[3])
                def _():
                    channels_sent(3, 2, 3)

            @pl.when(is_place[3] | (is_place[2] if group in high else place < 0))
            def _(group=group):
                merge(group)

            for part in members[group]:

                @pl.when(place > 0)
                def _(group=group, part=part):
                    if part == members[group][0]:
                        band_wait(early_slot, group_pieces[group])
                    band_wait(late_slot, part_pieces[part])

                attend(
                    *joined([in_slot(early_slot), in_slot(late_slot)]), 2 * band_keys,
                    mode="final", bounds=parts[part],
                )

        for role, index in ((0, 2), (1, 2), (2, 2)):

            @pl.when(is_place[role])
            def _(role=role, index=index):
                channels_sent(role, index)


def shards(tm_count, space_count, queries, key_rows, value_rows, block_list, block_count):
    rows, width = queries.shape
    blocks = rows // BLOCK
    picks = blocks // 2
    heads = width // HEAD
    slots = 2 * (tm_count.bit_length() - 1)
    kind = key_rows.dtype
    groups, parts, _ = head_groups(heads)
    in_hbm = pl.BlockSpec(memory_space=pltpu.HBM)
    dma = pltpu.SemaphoreType.DMA
    scratch = [
        pltpu.SMEM(block_list.shape, block_list.dtype),
        pltpu.SMEM(block_count.shape, block_count.dtype),
        pltpu.VMEM((rows, width), kind),
        pltpu.VMEM((rows, width), kind),
        pltpu.VMEM((rows, width), kind),
        pltpu.VMEM((2, BLOCK, width), kind),
        pltpu.VMEM((2, BLOCK, width), kind),
        pltpu.VMEM((slots, picks, BLOCK, width), kind),
        pltpu.VMEM((slots, picks, BLOCK, width), kind),
        pltpu.VMEM((heads, rows, HEAD), jnp.float32),
        pltpu.VMEM((heads, rows, HEAD), jnp.float32),
        pltpu.VMEM((heads, rows, HEAD), jnp.float32),
        pltpu.VMEM((blocks, (blocks + 2) * BLOCK), jnp.float32),
        pltpu.VMEM((slots, blocks, picks * BLOCK), jnp.float32),
        dma((5,)),
        dma((2,)),
        dma((2,)),
        dma((slots,)),
        dma((slots, len(parts))),
    ]
    if is_folded(tm_count):
        height = stat_height(heads)
        scratch += [
            pltpu.VMEM((2, rows, width), kind),
            pltpu.VMEM((2, rows, width), kind),
            pltpu.VMEM((4, blocks, picks * BLOCK), jnp.float32),
            pltpu.VMEM((2, len(groups), blocks, height, BLOCK), jnp.float32),
            pltpu.VMEM((len(groups), blocks, height, BLOCK), jnp.float32),
            dma((2,)),
            dma((2, len(groups))),
            dma((1,)),
            dma((2,)),
            dma((2,)),
            dma((len(groups),)),
        ]
    return pl.pallas_call(
        functools.partial(kernel, tm_count, space_count, block_list.shape[1]),
        out_shape=jax.ShapeDtypeStruct((rows, width), queries.dtype),
        in_specs=[in_hbm] * 5,
        out_specs=pl.BlockSpec(memory_space=pltpu.VMEM),
        scratch_shapes=scratch,
        compiler_params=pltpu.CompilerParams(
            collective_id=0, has_side_effects=True, vmem_limit_bytes=50 * 1024 * 1024
        ),
    )(*[
        pltpu.with_memory_space_constraint(array, pltpu.HBM)
        for array in (queries, key_rows, value_rows, block_list, block_count)
    ])


def solution(mesh):
    placed = (
        P(("tm", "space"), None),
        P(("tm", "space"), None),
        P(("tm", "space"), None),
        P(("tm", "space"), None),
        P(("tm", "space")),
    )
    return jax.shard_map(
        functools.partial(shards, mesh.shape["tm"], mesh.shape["space"]),
        mesh=mesh, in_specs=placed, out_specs=P(("tm", "space"), None), check_vma=False,
    )
```

```python
import functools
import math

import jax
import jax.numpy as jnp
from jax import lax
from jax.experimental import pallas as pl
from jax.experimental.pallas import tpu as pltpu
from jax.sharding import PartitionSpec as P

HEAD = 128
BLOCK = 128
LANES = 128
DEAD = -1e30
MESH = pl.DeviceIdType.MESH

TARGETS = {0: (1, 2, 3, 4), 1: (0, 2, 3, 5), 2: (3, 0, 1), 3: (2, 1, 7, 6)}


def head_groups(heads):
    quarter = max(1, heads // 4)
    groups = [(start, min(quarter, heads - start)) for start in range(0, heads, quarter)]
    parts, members = [], []
    for index, (start, count) in enumerate(groups):
        pieces = [(start, count)] if index < len(groups) - 1 else [(start + i, 1) for i in range(count)]
        members.append(list(range(len(parts), len(parts) + len(pieces))))
        parts += pieces
    return groups, parts, members


def stat_height(heads):
    return -(-2 * max(count for _, count in head_groups(heads)[0]) // 8) * 8


def landing_count(groups, parts, slots):
    return max(slots, 2 + len(parts) + 3 * len(groups))


def is_folded(tm_count):
    return tm_count.bit_length() - 1 == 3


def kernel(
    tm_count, space_count, list_width,
    q_hbm, k_hbm, v_hbm, list_hbm, count_hbm, o_ref,
    list_ref, count_ref,
    q_own, k_own, v_own, k_halo, v_halo, k_band, v_band,
    top, total, mixed, near_bias, band_bias,
    local_sem, halo_send, halo_recv, sent, landed,
    *guests,
):
    rows, width = q_hbm.shape
    blocks = rows // BLOCK
    picks = blocks // 2
    band_keys = picks * BLOCK
    heads = width // HEAD
    bits = tm_count.bit_length() - 1
    folded = is_folded(tm_count)
    groups, parts, members = head_groups(heads)
    all_parts = list(range(len(parts)))
    frame = lax.axis_index("tm")
    slab = lax.axis_index("space")
    scale = math.log2(math.e) / HEAD**0.5
    early = frame < tm_count // 2 if folded else frame >= 0
    place = jnp.where(early, frame, tm_count - 1 - frame)
    step = jnp.where(early, 1, -1)

    def flag(pred):
        return jnp.where(pred, 1, 0)

    def at(spot):
        return {"tm": jnp.where(early, spot, tm_count - 1 - spot)}

    def exists(delta):
        return (frame + delta >= 0) & (frame + delta < tm_count)

    def slab_exists(delta):
        return (slab + delta >= 0) & (slab + delta < space_count)

    def remote(src, dst, send_sem, recv_sem, device):
        return pltpu.make_async_remote_copy(
            src_ref=src, dst_ref=dst, send_sem=send_sem, recv_sem=recv_sem,
            device_id=device, device_id_type=MESH,
        )

    barrier = pltpu.get_barrier_semaphore()

    def greet(pred, device):
        @pl.when(pred)
        def _():
            pl.semaphore_signal(barrier, inc=1, device_id=device, device_id_type=MESH)

    expected = 0
    for delta in (-1, 1):
        expected = expected + flag(slab_exists(delta))
        greet(slab_exists(delta), {"space": slab + delta})
    if folded:
        last = tm_count - 1
        for role in TARGETS:
            expected = expected + jnp.where(place == role, len(TARGETS[role]), 0)
            for source, targets in TARGETS.items():
                if role in targets:
                    greet(place == role, at(source))
                if last - role in targets:
                    greet(place == role, at(last - source))
    else:
        for bit in range(bits):
            for delta in (1 << bit, -(1 << bit)):
                expected = expected + flag(exists(delta))
                greet(exists(delta), {"tm": frame + delta})
    def halo_copies(side, delta):
        start = (blocks - 1) * BLOCK if side == 0 else 0
        for src, dst in ((k_hbm, k_halo), (v_hbm, v_halo)):
            yield remote(
                src.at[pl.ds(start, BLOCK)], dst.at[side],
                halo_send.at[side], halo_recv.at[side], {"space": slab + delta},
            )

    def halo_wait(side, delta):
        return remote(k_halo, k_halo, halo_send.at[side], halo_recv.at[side], {"space": slab + delta})

    def columns(start, count):
        return pl.ds(start * HEAD, count * HEAD)

    whole = [(0, 0, heads)]
    group_pieces = [(members[i][0], *group) for i, group in enumerate(groups)]
    part_pieces = [(i, *part) for i, part in enumerate(parts)]

    def own_band(ref, parity):
        return ref.reshape(picks, 2, BLOCK, width).at[:, parity]

    first_early, first_late = 1, 1 + len(groups)
    first_extra = first_late + len(parts) + 1
    final_spot = len(parts) - 1

    def landing(role, slot, spot):
        group = [index for index, some in enumerate(members) if spot in some][0]
        if not folded:
            return slot
        if slot == 1 - role % 2:
            return 0
        if slot == (2 if role == 3 else 5):
            return first_early + group
        if slot == (1 if role % 2 else 3):
            return first_late + spot
        return first_extra + (group if role == 1 else 1 if slot == 0 else 0)

    def band_copies(channel, source, slot, pieces, device, role=None):
        kind, which = source
        for spot, start, count in pieces:
            cols = columns(start, count)
            for index, (own, near, band) in enumerate(((k_hbm, k_own, k_band), (v_hbm, v_own, v_band))):
                src = band.at[which] if kind == "band" else own_band(own if kind == "own" else near, which)
                apart = index if spot == final_spot else 0
                yield remote(
                    src.at[:, :, cols], band.at[slot].at[:, :, cols],
                    sent.at[channel], landed.at[landing(role, slot, spot) + apart], device,
                )

    def band_bytes(channel, where, count, kinds=2):
        some = k_band.at[pl.ds(0, kinds), :, :, columns(0, count)]
        return remote(some, some, sent.at[channel], landed.at[where], {"tm": frame})

    def band_wait(where, count, kinds=2):
        band_bytes(0, where, count, kinds).wait_recv()

    def sent_wait(channel, pieces):
        band_bytes(channel, 0, sum(piece[2] for piece in pieces)).wait_send()

    local = [
        pltpu.make_async_copy(src, dst, local_sem.at[index])
        for index, src, dst in (
            (0, list_hbm, list_ref), (1, count_hbm, count_ref),
            (2, q_hbm, q_own), (2, k_hbm, k_own), (2, v_hbm, v_own),
        )
    ]
    for copy in local:
        copy.start()

    def rows_wait():
        all_three = k_band.at[pl.ds(0, 6)]
        pltpu.make_async_copy(all_three, all_three, local_sem.at[2]).wait()

    def start_halos():
        for side, delta in ((0, 1), (1, -1)):

            @pl.when(slab_exists(delta))
            def _(side=side, delta=delta):
                for copy in halo_copies(side, delta):
                    copy.start()

    def halos_sent():
        for side, delta in ((0, 1), (1, -1)):

            @pl.when(slab_exists(delta))
            def _(side=side, delta=delta):
                halo_wait(side, delta).wait_send()

    frame_blocks = blocks * space_count
    first_block = frame * frame_blocks + slab * blocks

    def bias_rows(ids):
        row = jnp.concatenate([jnp.full((1, BLOCK), ident, jnp.int32) for ident in ids], axis=1)
        out = []
        for tile in range(blocks):
            count = count_ref[tile]
            value = jnp.full(row.shape, DEAD, jnp.float32)
            for entry in range(list_width):
                listed = jnp.where(entry < count, list_ref[tile, entry], -1)
                value = jnp.where(row == listed, 0.0, value)
            out.append(value)
        return out

    def fill_bias():
        for bit in range(bits):
            for side in (0, 1):
                partner = frame + (2 * side - 1) * step * (1 << bit)
                ids = [
                    partner * frame_blocks + slab * blocks + 2 * pick + bit % 2
                    for pick in range(picks)
                ]
                for tile, value in enumerate(bias_rows(ids)):
                    band_bias[2 * bit + side, tile : tile + 1, :] = value

    def fill_near():
        near_ids = [first_block + c for c in range(blocks)] + [first_block - 1, first_block + blocks]
        for tile, value in enumerate(bias_rows(near_ids)):
            near_bias[tile : tile + 1, :] = value

    def attend(get_k, get_v, get_bias, keys, mode="add", bounds=None, get_q=None, export=None):
        ones = jnp.ones((keys, HEAD), jnp.bfloat16)
        queries = get_q or (lambda cols: q_own[:, cols])

        def one_head(head, carry):
            cols = pl.ds(pl.multiple_of(head * HEAD, HEAD), HEAD)
            raw = lax.dot_general(
                queries(cols), get_k(cols), (((1,), (1,)), ((), ())),
                preferred_element_type=jnp.float32,
            )
            weights, shrink, tops = [], [], []
            for tile in range(blocks):
                span = slice(tile * BLOCK, (tile + 1) * BLOCK)
                scores = raw[span] * scale + get_bias(tile)
                peak = jnp.max(scores, axis=1, keepdims=True)
                if mode in ("first", "export"):
                    new_top = jnp.broadcast_to(peak, (BLOCK, HEAD))
                else:
                    old_top = top[head, span, :]
                    new_top = jnp.maximum(old_top, peak)
                    shrink.append(jnp.exp2(old_top - new_top))
                if mode in ("first", "add"):
                    top[head, span, :] = new_top
                tops.append(new_top)
                wide = jnp.concatenate([new_top] * (keys // HEAD), axis=1)
                weights.append(jnp.exp2(scores - wide).astype(jnp.bfloat16))
            extended = jnp.concatenate([get_v(cols), ones], axis=1)
            both = jnp.dot(
                jnp.concatenate(weights, axis=0), extended, preferred_element_type=jnp.float32
            )
            if mode == "export":
                export(head, cols, both[:, :HEAD], tops, both[:, HEAD:])
            elif mode == "first":
                mixed[head] = both[:, :HEAD]
                total[head] = both[:, HEAD:]
            else:
                factor = jnp.concatenate(shrink, axis=0)
                new_mixed = mixed[head] * factor + both[:, :HEAD]
                new_total = total[head] * factor + both[:, HEAD:]
                if mode == "final":
                    o_ref[:, cols] = (new_mixed / new_total).astype(o_ref.dtype)
                else:
                    mixed[head] = new_mixed
                    total[head] = new_total
            return carry

        start, count = (0, heads) if bounds is None else bounds
        paired = count - count % 2
        if export is not None:
            paired = 0
        if paired > 2:
            lax.fori_loop(start, start + paired, one_head, 0, unroll=2)
        for head in range(start if paired <= 2 else start + paired, start + count):
            one_head(head, 0)

    def attend_own():
        attend(
            lambda cols: k_own[:, cols],
            lambda cols: v_own[:, cols],
            lambda tile: near_bias[tile : tile + 1, : blocks * BLOCK],
            blocks * BLOCK,
            mode="first",
        )

    def attend_halos():
        for side, delta in ((0, -1), (1, 1)):

            @pl.when(slab_exists(delta))
            def _(side=side, delta=delta):
                halo_wait(side, delta).wait_recv()
                start = (blocks + side) * BLOCK
                attend(
                    lambda cols: k_halo[side, :, cols],
                    lambda cols: v_halo[side, :, cols],
                    lambda tile: near_bias[tile : tile + 1, start : start + BLOCK],
                    BLOCK,
                )

    def in_slot(slot):
        return (
            lambda cols: k_band[slot, :, :, cols].reshape(band_keys, HEAD),
            lambda cols: v_band[slot, :, :, cols].reshape(band_keys, HEAD),
            lambda tile: band_bias[slot, tile : tile + 1, :],
        )

    def joined(sources):
        def join(index, axis):
            return lambda arg: jnp.concatenate([s[index](arg) for s in sources], axis=axis)

        return join(0, 0), join(1, 0), join(2, 1)

    for copy in local[:2]:
        copy.wait()
    fill_bias()
    fill_near()
    pl.semaphore_wait(barrier, expected)

    if not folded:
        start_halos()
        for bit in list(range(1, bits)) + [0]:
            for side, delta in ((0, 1 << bit), (1, -(1 << bit))):

                @pl.when(exists(delta))
                def _(bit=bit, side=side, delta=delta):
                    slot = 2 * bit + side
                    for copy in band_copies(slot, ("own", bit % 2), slot, whole, {"tm": frame + delta}):
                        copy.start()

        rows_wait()
        attend_own()
        attend_halos()
        for bit in list(range(1, bits)) + [0]:
            for side, delta in ((0, -(1 << bit)), (1, 1 << bit)):

                @pl.when(exists(delta))
                def _(bit=bit, side=side):
                    slot = 2 * bit + side
                    band_wait(slot, heads)
                    attend(*in_slot(slot), band_keys)

        def finish(head, carry):
            cols = pl.ds(pl.multiple_of(head * HEAD, HEAD), HEAD)
            o_ref[:, cols] = (mixed[head] / total[head]).astype(o_ref.dtype)
            return carry

        lax.fori_loop(0, heads, finish, 0)
        for bit in range(bits):
            for side, delta in ((0, 1 << bit), (1, -(1 << bit))):

                @pl.when(exists(delta))
                def _(slot=2 * bit + side):
                    sent_wait(slot, whole)

        halos_sent()

    else:
        (
            guest, away, guest_bias, stat_out, stat_in,
        ) = guests
        first_guest_sent, first_stat_sent = 3, 5
        query_sent, bias_sent = 4, 5
        upper = len(groups) // 2
        every, high = range(len(groups)), range(upper, len(groups))
        low_pieces = group_pieces[:upper]
        low_span = (0, groups[upper][0])

        channels = {
            0: [
                (("own", 0), 1, 0, whole),
                (("own", 1), 2, 2, low_pieces),
                (("band", 5), 3, 1, part_pieces),
            ],
            1: [
                (("own", 0), 0, 1, whole),
                (("own", 0), 2, 0, low_pieces),
                (("own", 1), 3, 2, group_pieces),
                (("own", 0), 5, 5, group_pieces),
                (("band", 3), 5, 3, part_pieces),
            ],
            2: [
                (("own", 0), 3, 0, whole),
                (("own", 1), 0, 3, group_pieces),
                (("near", 0), 1, 1, part_pieces),
            ],
            3: [
                (("own", 0), 2, 1, whole),
                (("own", 1), 1, 3, group_pieces),
                (("near", 0), 7, 5, group_pieces),
                (("band", 0), 6, 5, group_pieces),
            ],
        }

        def start_channel(role, index, spots=None):
            source, target, slot, pieces = channels[role][index]
            pieces = [piece for piece in pieces if spots is None or piece[0] in spots]
            role_there = min(target, tm_count - 1 - target)
            for copy in band_copies(index, source, slot, pieces, at(target), role_there):
                copy.start()

        def channels_sent(role, *indices):
            for index in indices:
                sent_wait(index, channels[role][index][3])

        guest_groups = (every, high)
        guest_host = (7, 0)
        guest_home = (4, 2)
        guest_slots = ((5, 3), (2, 0))

        def query_landing(index, group):
            return first_extra + group + (0 if index == 0 else len(groups) - upper)

        def query_copy(index, group):
            cols = columns(*groups[group])
            return remote(
                q_hbm.at[:, cols], guest.at[index, :, cols],
                sent.at[query_sent], landed.at[query_landing(index, group)], at(guest_host[index]),
            )

        def guest_wait_sent(index, channel):
            cols = columns(0, sum(groups[group][1] for group in guest_groups[index]))
            ref = guest.at[index, :, cols]
            remote(ref, ref, sent.at[channel], landed.at[0], {"tm": frame}).wait_send()

        def bias_landing(index):
            return first_extra + 2 * len(groups) - 2 + index

        def bias_copy(index, which):
            return remote(
                band_bias.at[guest_slots[index][which]], guest_bias.at[2 * index + which],
                sent.at[bias_sent], landed.at[bias_landing(index)], at(guest_host[index]),
            )

        def bias_wait(index):
            pair = guest_bias.at[pl.ds(2 * index, 2)]
            return remote(pair, pair, sent.at[bias_sent], landed.at[bias_landing(index)], {"tm": frame})

        def result_copy(index, group):
            cols = columns(*groups[group])
            return remote(
                away.at[index, :, cols], guest.at[0, :, cols],
                sent.at[first_guest_sent + index], landed.at[first_extra + group], at(guest_home[index]),
            )

        def stat_copy(index, group):
            return remote(
                stat_out.at[index, group], stat_in.at[group],
                sent.at[first_stat_sent + index], landed.at[first_extra + len(groups) + group],
                at(guest_home[index]),
            )

        def results_sent(index):
            guest_wait_sent(index, first_guest_sent + index)
            ref = stat_out.at[index, pl.ds(0, len(guest_groups[index]))]
            remote(ref, ref, sent.at[first_stat_sent + index], landed.at[0], {"tm": frame}).wait_send()

        def queries_sent(index):
            guest_wait_sent(index, query_sent)
            bias_wait(index).wait_send()

        height = stat_height(heads)

        def host(index, group, sources):
            held = []

            def export(head, cols, value, tops, sums):
                away[index, :, cols] = value.astype(away.dtype)
                held.append((tops, sums))

            attend(
                *joined(sources), 2 * band_keys, mode="export", bounds=groups[group],
                get_q=lambda cols: guest[index, :, cols], export=export,
            )
            result_copy(index, group).start()
            lane = lax.broadcasted_iota(jnp.int32, (BLOCK, LANES), 1)
            for tile in range(blocks):
                packed = jnp.zeros((BLOCK, LANES), jnp.float32)
                for place_in, (tops, sums) in enumerate(held):
                    span = slice(tile * BLOCK, (tile + 1) * BLOCK)
                    packed = jnp.where(lane == 2 * place_in, tops[tile], packed)
                    packed = jnp.where(lane == 2 * place_in + 1, sums[span], packed)
                stat_out[index, group, tile] = jnp.transpose(packed)[:height]
            stat_copy(index, group).start()

        def host_source(index, which, parity=None, slot=None):
            def bias(tile):
                return guest_bias[2 * index + which, tile : tile + 1, :]

            if slot is not None:
                get_k, get_v, _ = in_slot(slot)
                return get_k, get_v, bias

            def own(ref):
                return lambda cols: jnp.concatenate(
                    [ref[pl.ds((2 * pick + parity) * BLOCK, BLOCK), cols] for pick in range(picks)], axis=0
                )

            return own(k_own), own(v_own), bias

        def merge(group):
            start, count = groups[group]
            result_copy(0, group).wait_recv()
            stat_copy(0, group).wait_recv()

            def one_tile(tile, carry):
                span = pl.ds(pl.multiple_of(tile * BLOCK, BLOCK), BLOCK)
                packed = jnp.concatenate(
                    [stat_in[group, tile], jnp.zeros((LANES - height, BLOCK), jnp.float32)], axis=0
                )
                stats = jnp.transpose(packed)
                for index in range(count):
                    head = start + index
                    their_top = jnp.broadcast_to(stats[:, 2 * index : 2 * index + 1], (BLOCK, HEAD))
                    their_sum = jnp.broadcast_to(stats[:, 2 * index + 1 : 2 * index + 2], (BLOCK, HEAD))
                    old_top = top[head, span, :]
                    new_top = jnp.maximum(old_top, their_top)
                    ours, theirs = jnp.exp2(old_top - new_top), jnp.exp2(their_top - new_top)
                    value = guest[0, span, columns(head, 1)].astype(jnp.float32)
                    top[head, span, :] = new_top
                    mixed[head, span, :] = mixed[head, span, :] * ours + value * theirs
                    total[head, span, :] = total[head, span, :] * ours + their_sum * theirs
                return carry

            lax.fori_loop(0, blocks, one_tile, 0)

        is_place = [place == role for role in range(4)]

        @pl.when(is_place[0])
        def _():
            start_channel(0, 1)
            start_channel(0, 0)

        @pl.when(is_place[1])
        def _():
            for index in (1, 3, 0, 2):
                start_channel(1, index)

        @pl.when(is_place[2])
        def _():
            for group in high:
                query_copy(1, group).start()
            for which in (0, 1):
                bias_copy(1, which).start()
            start_channel(2, 0)
            start_channel(2, 1)

        @pl.when(is_place[3])
        def _():
            start_channel(3, 1)
            for group in every:
                query_copy(0, group).start()
            for which in (0, 1):
                bias_copy(0, which).start()
            start_channel(3, 0)

        start_halos()

        rows_wait()

        @pl.when(is_place[2])
        def _():
            start_channel(2, 2)

        @pl.when(is_place[3])
        def _():
            start_channel(3, 2)

        attend_own()

        beside = 1 - lax.rem(place, 2)
        band_wait(0, heads)

        @pl.when(is_place[3])
        def _():
            start_channel(3, 3)

        def relay(role, channel, slot, group):
            band_wait(landing(role, slot, members[group][0]), groups[group][1])
            start_channel(role, channel, members[group])

        @pl.when(is_place[1])
        def _():
            relay(1, 4, 3, 0)

        attend(*in_slot(beside), band_keys)

        @pl.when(is_place[0])
        def _():
            bias_wait(1).wait_recv()
            for group in high:
                query_copy(1, group).wait_recv()
                host(1, group, [host_source(1, 0, parity=1), host_source(1, 1, slot=1)])

        @pl.when(is_place[1])
        def _():
            relay(1, 4, 3, 1)

        attend_halos()

        @pl.when(is_place[0])
        def _():
            bias_wait(0).wait_recv()
            for group in every:
                relay(0, 2, 5, group)
                query_copy(0, group).wait_recv()
                band_wait(landing(0, 3, members[group][0]), groups[group][1])
                host(0, group, [host_source(0, 0, parity=0), host_source(0, 1, slot=3)])
            channels_sent(0, 0, 1)
            results_sent(1)

        @pl.when(is_place[1])
        def _():
            for group in every[2:]:
                relay(1, 4, 3, group)
            attend(*in_slot(3), band_keys)
            channels_sent(1, 0, 1, 3)

        @pl.when(is_place[2])
        def _():
            for slot in (2, 0):
                band_wait(landing(2, slot, 0), low_span[1])
            attend(*joined([in_slot(2), in_slot(0)]), 2 * band_keys, bounds=low_span)
            queries_sent(1)
            channels_sent(2, 0)

        @pl.when(is_place[3])
        def _():
            queries_sent(0)
            channels_sent(3, 0, 1)

        halos_sent()
        early_slot = jnp.where(is_place[3], 2, 5)
        late_slot = jnp.where(lax.rem(place, 2) == 0, 3, 1)

        def wait_early(group):
            @pl.when(place > 0)
            def _():
                band_wait(first_early + group, groups[group][1])

        def wait_late(part, kinds=2, apart=0):
            @pl.when(place > 0)
            def _():
                band_wait(first_late + part + apart, parts[part][1], kinds)

        def merge_there(group):
            @pl.when(is_place[3] | (is_place[2] if group in high else place < 0))
            def _():
                merge(group)

        get_k, get_v, get_bias = in_slot(late_slot)
        final_group = len(groups) - 1
        for group in every:
            if group == 0:
                merge_there(0)
                wait_early(final_group)
                attend(*in_slot(early_slot), band_keys, bounds=groups[final_group])
            if group < final_group:
                wait_early(group)
                for part in members[group]:
                    wait_late(part)
                    attend(
                        *joined([in_slot(early_slot), in_slot(late_slot)]), 2 * band_keys,
                        mode="final", bounds=parts[part],
                    )
                merge_there(group + 1)
                continue

            @pl.when(is_place[0])
            def _():
                results_sent(0)

            @pl.when(is_place[1])
            def _():
                channels_sent(1, 4)

            @pl.when(is_place[2])
            def _():
                channels_sent(2, 1)

            @pl.when(is_place[3])
            def _():
                channels_sent(3, 2, 3)

            for part in members[group]:
                last_part = part == final_spot

                def values(cols, part=part, last_part=last_part):
                    if last_part:
                        wait_late(part, kinds=1, apart=1)
                    return get_v(cols)

                wait_late(part, kinds=1 if last_part else 2)
                attend(get_k, values, get_bias, band_keys, mode="final", bounds=parts[part])

        for role, index in ((0, 2), (1, 2), (2, 2)):

            @pl.when(is_place[role])
            def _(role=role, index=index):
                channels_sent(role, index)


def shards(tm_count, space_count, queries, key_rows, value_rows, block_list, block_count):
    rows, width = queries.shape
    blocks = rows // BLOCK
    picks = blocks // 2
    heads = width // HEAD
    slots = 2 * (tm_count.bit_length() - 1)
    kind = key_rows.dtype
    groups, parts, _ = head_groups(heads)
    in_hbm = pl.BlockSpec(memory_space=pltpu.HBM)
    dma = pltpu.SemaphoreType.DMA
    scratch = [
        pltpu.SMEM(block_list.shape, block_list.dtype),
        pltpu.SMEM(block_count.shape, block_count.dtype),
        pltpu.VMEM((rows, width), kind),
        pltpu.VMEM((rows, width), kind),
        pltpu.VMEM((rows, width), kind),
        pltpu.VMEM((2, BLOCK, width), kind),
        pltpu.VMEM((2, BLOCK, width), kind),
        pltpu.VMEM((slots, picks, BLOCK, width), kind),
        pltpu.VMEM((slots, picks, BLOCK, width), kind),
        pltpu.VMEM((heads, rows, HEAD), jnp.float32),
        pltpu.VMEM((heads, rows, HEAD), jnp.float32),
        pltpu.VMEM((heads, rows, HEAD), jnp.float32),
        pltpu.VMEM((blocks, (blocks + 2) * BLOCK), jnp.float32),
        pltpu.VMEM((slots, blocks, picks * BLOCK), jnp.float32),
        dma((3,)),
        dma((2,)),
        dma((2,)),
        dma((max(7, slots),)),
        dma((landing_count(groups, parts, slots),)),
    ]
    if is_folded(tm_count):
        height = stat_height(heads)
        scratch += [
            pltpu.VMEM((2, rows, width), kind),
            pltpu.VMEM((2, rows, width), kind),
            pltpu.VMEM((4, blocks, picks * BLOCK), jnp.float32),
            pltpu.VMEM((2, len(groups), blocks, height, BLOCK), jnp.float32),
            pltpu.VMEM((len(groups), blocks, height, BLOCK), jnp.float32),
        ]
    return pl.pallas_call(
        functools.partial(kernel, tm_count, space_count, block_list.shape[1]),
        out_shape=jax.ShapeDtypeStruct((rows, width), queries.dtype),
        in_specs=[in_hbm] * 5,
        out_specs=pl.BlockSpec(memory_space=pltpu.VMEM),
        scratch_shapes=scratch,
        compiler_params=pltpu.CompilerParams(
            collective_id=0, has_side_effects=True, vmem_limit_bytes=50 * 1024 * 1024
        ),
    )(*[
        pltpu.with_memory_space_constraint(array, pltpu.HBM)
        for array in (queries, key_rows, value_rows, block_list, block_count)
    ])


def solution(mesh):
    placed = (
        P(("tm", "space"), None),
        P(("tm", "space"), None),
        P(("tm", "space"), None),
        P(("tm", "space"), None),
        P(("tm", "space")),
    )
    return jax.shard_map(
        functools.partial(shards, mesh.shape["tm"], mesh.shape["space"]),
        mesh=mesh, in_specs=placed, out_specs=P(("tm", "space"), None), check_vma=False,
    )
```

```python
import functools
import math

import jax
import jax.numpy as jnp
from jax import lax
from jax.experimental import pallas as pl
from jax.experimental.pallas import tpu as pltpu
from jax.sharding import PartitionSpec as P

HEAD = 128
BLOCK = 128
LANES = 128
DEAD = -1e30
MESH = pl.DeviceIdType.MESH

def head_groups(heads):
    quarter = max(1, heads // 4)
    groups = [(start, min(quarter, heads - start)) for start in range(0, heads, quarter)]
    parts, members = [], []
    for index, (start, count) in enumerate(groups):
        pieces = [(start, count)] if index < len(groups) - 1 else [(start + i, 1) for i in range(count)]
        members.append(list(range(len(parts), len(parts) + len(pieces))))
        parts += pieces
    return groups, parts, members


def stat_height(heads):
    return -(-2 * max(count for _, count in head_groups(heads)[0]) // 8) * 8


def landing_count(groups, parts, slots):
    return max(slots, 2 + len(parts) + 3 * len(groups))


def is_folded(tm_count):
    return tm_count.bit_length() - 1 == 3


def kernel(
    tm_count, space_count, list_width,
    q_hbm, k_hbm, v_hbm, list_hbm, count_hbm, o_ref,
    list_ref, count_ref,
    q_own, k_own, v_own, k_halo, v_halo, k_band, v_band,
    top, total, mixed, near_bias, band_bias,
    local_sem, halo_send, halo_recv, sent, landed,
    *guests,
):
    rows, width = q_hbm.shape
    blocks = rows // BLOCK
    picks = blocks // 2
    band_keys = picks * BLOCK
    heads = width // HEAD
    bits = tm_count.bit_length() - 1
    folded = is_folded(tm_count)
    groups, parts, members = head_groups(heads)
    all_parts = list(range(len(parts)))
    frame = lax.axis_index("tm")
    slab = lax.axis_index("space")
    scale = math.log2(math.e) / HEAD**0.5
    early = frame < tm_count // 2 if folded else frame >= 0
    place = jnp.where(early, frame, tm_count - 1 - frame)
    step = jnp.where(early, 1, -1)

    def flag(pred):
        return jnp.where(pred, 1, 0)

    def at(spot):
        return {"tm": jnp.where(early, spot, tm_count - 1 - spot)}

    def exists(delta):
        return (frame + delta >= 0) & (frame + delta < tm_count)

    def slab_exists(delta):
        return (slab + delta >= 0) & (slab + delta < space_count)

    def remote(src, dst, send_sem, recv_sem, device):
        return pltpu.make_async_remote_copy(
            src_ref=src, dst_ref=dst, send_sem=send_sem, recv_sem=recv_sem,
            device_id=device, device_id_type=MESH,
        )

    barrier = pltpu.get_barrier_semaphore()

    def greet(pred, device):
        @pl.when(pred)
        def _():
            pl.semaphore_signal(barrier, inc=1, device_id=device, device_id_type=MESH)

    even = lax.rem(place, 2) == 0
    odd = jnp.logical_not(even)
    outer = place < 2
    odd_spot = place + 1 - lax.rem(place, 2)
    partner = at(place + 1 - 2 * lax.rem(place, 2))
    expected = 0
    if folded:
        greet(outer, at(2))
        greet(jnp.logical_not(outer), at(0))
        greet(odd, partner)
        greet(outer, at(4))
        greet(jnp.logical_not(outer), at(6))
        expected = 2
        for delta in (-1, 1):
            greet(slab_exists(delta), {"space": slab + delta, **at(odd_spot)})
            expected = expected + 2 * flag(slab_exists(delta))
    else:
        for delta in (-1, 1):
            expected = expected + flag(slab_exists(delta))
            greet(slab_exists(delta), {"space": slab + delta})
        for bit in range(bits):
            for delta in (1 << bit, -(1 << bit)):
                expected = expected + flag(exists(delta))
                greet(exists(delta), {"tm": frame + delta})

    def halo_copies(side, delta):
        start = (blocks - 1) * BLOCK if side == 0 else 0
        for src, dst in ((k_hbm, k_halo), (v_hbm, v_halo)):
            yield remote(
                src.at[pl.ds(start, BLOCK)], dst.at[side],
                halo_send.at[side], halo_recv.at[side], {"space": slab + delta},
            )

    def halo_wait(side, delta):
        return remote(k_halo, k_halo, halo_send.at[side], halo_recv.at[side], {"space": slab + delta})

    def columns(start, count):
        return pl.ds(start * HEAD, count * HEAD)

    whole = [(0, 0, heads)]
    group_pieces = [(members[i][0], *group) for i, group in enumerate(groups)]
    part_pieces = [(i, *part) for i, part in enumerate(parts)]

    def own_band(ref, parity):
        return ref.reshape(picks, 2, BLOCK, width).at[:, parity]

    first_early, first_late = 1, 1 + len(groups)
    first_extra = first_late + len(parts) + 1
    final_spot = len(parts) - 1

    def landing(role, slot, spot):
        group = [index for index, some in enumerate(members) if spot in some][0]
        if not folded:
            return slot
        if slot == 1 - role % 2:
            return 0
        if slot == (2 if role == 3 else 5):
            return first_early + group
        if slot == (1 if role % 2 else 3):
            return first_late + spot
        return first_extra + (group if role == 1 else 1 if slot == 0 else 0)

    def band_copies(channel, source, slot, pieces, device, role=None):
        kind, which = source
        for spot, start, count in pieces:
            cols = columns(start, count)
            for index, (own, near, band) in enumerate(((k_hbm, k_own, k_band), (v_hbm, v_own, v_band))):
                src = band.at[which] if kind == "band" else own_band(own if kind == "own" else near, which)
                apart = index if spot == final_spot else 0
                yield remote(
                    src.at[:, :, cols], band.at[slot].at[:, :, cols],
                    sent.at[channel], landed.at[landing(role, slot, spot) + apart], device,
                )

    def band_bytes(channel, where, count, kinds=2):
        some = k_band.at[pl.ds(0, kinds), :, :, columns(0, count)]
        return remote(some, some, sent.at[channel], landed.at[where], {"tm": frame})

    def band_wait(where, count, kinds=2):
        band_bytes(0, where, count, kinds).wait_recv()

    def sent_wait(channel, pieces):
        band_bytes(channel, 0, sum(piece[2] for piece in pieces)).wait_send()

    local = [
        pltpu.make_async_copy(src, dst, local_sem.at[index])
        for index, src, dst in (
            (0, list_hbm, list_ref), (1, count_hbm, count_ref),
            (2, q_hbm, q_own), (2, k_hbm, k_own), (2, v_hbm, v_own),
        )
    ]
    for copy in local:
        copy.start()

    def rows_wait():
        all_three = k_band.at[pl.ds(0, 6)]
        pltpu.make_async_copy(all_three, all_three, local_sem.at[2]).wait()

    def start_halos():
        for side, delta in ((0, 1), (1, -1)):

            @pl.when(slab_exists(delta))
            def _(side=side, delta=delta):
                for copy in halo_copies(side, delta):
                    copy.start()

    def halos_sent():
        for side, delta in ((0, 1), (1, -1)):

            @pl.when(slab_exists(delta))
            def _(side=side, delta=delta):
                halo_wait(side, delta).wait_send()

    frame_blocks = blocks * space_count
    first_block = frame * frame_blocks + slab * blocks

    def bias_rows(ids):
        row = jnp.concatenate([jnp.full((1, BLOCK), ident, jnp.int32) for ident in ids], axis=1)
        out = []
        for tile in range(blocks):
            count = count_ref[tile]
            value = jnp.full(row.shape, DEAD, jnp.float32)
            for entry in range(list_width):
                listed = jnp.where(entry < count, list_ref[tile, entry], -1)
                value = jnp.where(row == listed, 0.0, value)
            out.append(value)
        return out

    def fill_bias():
        for bit in range(bits):
            for side in (0, 1):
                partner = frame + (2 * side - 1) * step * (1 << bit)
                ids = [
                    partner * frame_blocks + slab * blocks + 2 * pick + bit % 2
                    for pick in range(picks)
                ]
                for tile, value in enumerate(bias_rows(ids)):
                    band_bias[2 * bit + side, tile : tile + 1, :] = value

    def fill_near():
        near_ids = [first_block + c for c in range(blocks)] + [first_block - 1, first_block + blocks]
        for tile, value in enumerate(bias_rows(near_ids)):
            near_bias[tile : tile + 1, :] = value

    def attend(get_k, get_v, get_bias, keys, mode="add", bounds=None, get_q=None, export=None):
        ones = jnp.ones((keys, HEAD), jnp.bfloat16)
        queries = get_q or (lambda cols: q_own[:, cols])

        def one_head(head, carry):
            cols = pl.ds(pl.multiple_of(head * HEAD, HEAD), HEAD)
            raw = lax.dot_general(
                queries(cols), get_k(cols), (((1,), (1,)), ((), ())),
                preferred_element_type=jnp.float32,
            )
            weights, shrink, tops = [], [], []
            for tile in range(blocks):
                span = slice(tile * BLOCK, (tile + 1) * BLOCK)
                scores = raw[span] * scale + get_bias(tile)
                peak = jnp.max(scores, axis=1, keepdims=True)
                if mode in ("first", "export"):
                    new_top = jnp.broadcast_to(peak, (BLOCK, HEAD))
                else:
                    old_top = top[head, span, :]
                    new_top = jnp.maximum(old_top, peak)
                    shrink.append(jnp.exp2(old_top - new_top))
                if mode in ("first", "add"):
                    top[head, span, :] = new_top
                tops.append(new_top)
                wide = jnp.concatenate([new_top] * (keys // HEAD), axis=1)
                weights.append(jnp.exp2(scores - wide).astype(jnp.bfloat16))
            extended = jnp.concatenate([get_v(cols), ones], axis=1)
            both = jnp.dot(
                jnp.concatenate(weights, axis=0), extended, preferred_element_type=jnp.float32
            )
            if mode == "export":
                export(head, cols, both[:, :HEAD], tops, both[:, HEAD:])
            elif mode == "first":
                mixed[head] = both[:, :HEAD]
                total[head] = both[:, HEAD:]
            else:
                factor = jnp.concatenate(shrink, axis=0)
                new_mixed = mixed[head] * factor + both[:, :HEAD]
                new_total = total[head] * factor + both[:, HEAD:]
                if mode == "final":
                    o_ref[:, cols] = (new_mixed / new_total).astype(o_ref.dtype)
                else:
                    mixed[head] = new_mixed
                    total[head] = new_total
            return carry

        start, count = (0, heads) if bounds is None else bounds
        paired = count - count % 2
        if export is not None:
            paired = 0
        if paired > 2:
            lax.fori_loop(start, start + paired, one_head, 0, unroll=2)
        for head in range(start if paired <= 2 else start + paired, start + count):
            one_head(head, 0)

    def attend_own():
        attend(
            lambda cols: k_own[:, cols],
            lambda cols: v_own[:, cols],
            lambda tile: near_bias[tile : tile + 1, : blocks * BLOCK],
            blocks * BLOCK,
            mode="first",
        )

    def attend_halos():
        for side, delta in ((0, -1), (1, 1)):

            @pl.when(slab_exists(delta))
            def _(side=side, delta=delta):
                halo_wait(side, delta).wait_recv()
                start = (blocks + side) * BLOCK
                attend(
                    lambda cols: k_halo[side, :, cols],
                    lambda cols: v_halo[side, :, cols],
                    lambda tile: near_bias[tile : tile + 1, start : start + BLOCK],
                    BLOCK,
                )

    def in_slot(slot):
        return (
            lambda cols: k_band[slot, :, :, cols].reshape(band_keys, HEAD),
            lambda cols: v_band[slot, :, :, cols].reshape(band_keys, HEAD),
            lambda tile: band_bias[slot, tile : tile + 1, :],
        )

    def joined(sources):
        def join(index, axis):
            return lambda arg: jnp.concatenate([s[index](arg) for s in sources], axis=axis)

        return join(0, 0), join(1, 0), join(2, 1)

    def fill():
        for copy in local[:2]:
            copy.wait()
        fill_bias()
        fill_near()

    if not folded:
        fill()
        pl.semaphore_wait(barrier, expected)
        start_halos()
        for bit in list(range(1, bits)) + [0]:
            for side, delta in ((0, 1 << bit), (1, -(1 << bit))):

                @pl.when(exists(delta))
                def _(bit=bit, side=side, delta=delta):
                    slot = 2 * bit + side
                    for copy in band_copies(slot, ("own", bit % 2), slot, whole, {"tm": frame + delta}):
                        copy.start()

        rows_wait()
        attend_own()
        attend_halos()
        for bit in list(range(1, bits)) + [0]:
            for side, delta in ((0, -(1 << bit)), (1, 1 << bit)):

                @pl.when(exists(delta))
                def _(bit=bit, side=side):
                    slot = 2 * bit + side
                    band_wait(slot, heads)
                    attend(*in_slot(slot), band_keys)

        def finish(head, carry):
            cols = pl.ds(pl.multiple_of(head * HEAD, HEAD), HEAD)
            o_ref[:, cols] = (mixed[head] / total[head]).astype(o_ref.dtype)
            return carry

        lax.fori_loop(0, heads, finish, 0)
        for bit in range(bits):
            for side, delta in ((0, 1 << bit), (1, -(1 << bit))):

                @pl.when(exists(delta))
                def _(slot=2 * bit + side):
                    sent_wait(slot, whole)

        halos_sent()

    else:
        (
            guest, away, guest_bias, stat_out, stat_in, ready,
        ) = guests
        first_guest_sent, first_stat_sent = 3, 5
        query_sent, bias_sent = 4, 5
        upper = len(groups) // 2
        every, high = range(len(groups)), range(upper, len(groups))
        low_pieces = group_pieces[:upper]
        low_span = (0, groups[upper][0])

        channels = {
            0: [
                (("own", 0), 1, 0, whole),
                (("own", 1), 2, 2, low_pieces),
                (("band", 5), 3, 1, part_pieces),
            ],
            1: [
                (("own", 0), 0, 1, whole),
                (("own", 0), 2, 0, low_pieces),
                (("own", 1), 3, 2, group_pieces),
                (("own", 0), 5, 5, group_pieces),
                (("band", 3), 5, 3, part_pieces),
            ],
            2: [
                (("own", 0), 3, 0, whole),
                (("own", 1), 0, 3, group_pieces),
                (("near", 0), 1, 1, part_pieces),
            ],
            3: [
                (("own", 0), 2, 1, whole),
                (("own", 1), 1, 3, group_pieces),
                (("near", 0), 7, 5, group_pieces),
                (("band", 0), 6, 5, group_pieces),
            ],
        }

        def start_channel(role, index, spots=None):
            source, target, slot, pieces = channels[role][index]
            pieces = [piece for piece in pieces if spots is None or piece[0] in spots]
            role_there = min(target, tm_count - 1 - target)
            for copy in band_copies(index, source, slot, pieces, at(target), role_there):
                copy.start()

        def channels_sent(role, *indices):
            for index in indices:
                sent_wait(index, channels[role][index][3])

        guest_groups = (every, high)
        guest_host = (7, 0)
        guest_home = (4, 2)
        guest_slots = ((5, 3), (2, 0))

        def query_landing(index, group):
            return first_extra + group + (0 if index == 0 else len(groups) - upper)

        def query_copy(index, group):
            cols = columns(*groups[group])
            return remote(
                q_hbm.at[:, cols], guest.at[index, :, cols],
                sent.at[query_sent], landed.at[query_landing(index, group)], at(guest_host[index]),
            )

        def guest_wait_sent(index, channel):
            cols = columns(0, sum(groups[group][1] for group in guest_groups[index]))
            ref = guest.at[index, :, cols]
            remote(ref, ref, sent.at[channel], landed.at[0], {"tm": frame}).wait_send()

        def bias_landing(index):
            return first_extra + 2 * len(groups) - 2 + index

        def bias_copy(index, which):
            return remote(
                band_bias.at[guest_slots[index][which]], guest_bias.at[2 * index + which],
                sent.at[bias_sent], landed.at[bias_landing(index)], at(guest_host[index]),
            )

        def bias_wait(index):
            pair = guest_bias.at[pl.ds(2 * index, 2)]
            return remote(pair, pair, sent.at[bias_sent], landed.at[bias_landing(index)], {"tm": frame})

        def result_copy(index, group):
            cols = columns(*groups[group])
            return remote(
                away.at[index, :, cols], guest.at[0, :, cols],
                sent.at[first_guest_sent + index], landed.at[first_extra + group], at(guest_home[index]),
            )

        def stat_copy(index, group):
            return remote(
                stat_out.at[index, group], stat_in.at[group],
                sent.at[first_stat_sent + index], landed.at[first_extra + len(groups) + group],
                at(guest_home[index]),
            )

        def results_sent(index):
            guest_wait_sent(index, first_guest_sent + index)
            ref = stat_out.at[index, pl.ds(0, len(guest_groups[index]))]
            remote(ref, ref, sent.at[first_stat_sent + index], landed.at[0], {"tm": frame}).wait_send()

        def queries_sent(index):
            guest_wait_sent(index, query_sent)
            bias_wait(index).wait_send()

        height = stat_height(heads)

        def host(index, group, sources):
            held = []

            def export(head, cols, value, tops, sums):
                away[index, :, cols] = value.astype(away.dtype)
                held.append((tops, sums))

            attend(
                *joined(sources), 2 * band_keys, mode="export", bounds=groups[group],
                get_q=lambda cols: guest[index, :, cols], export=export,
            )
            result_copy(index, group).start()
            lane = lax.broadcasted_iota(jnp.int32, (BLOCK, LANES), 1)
            for tile in range(blocks):
                packed = jnp.zeros((BLOCK, LANES), jnp.float32)
                for place_in, (tops, sums) in enumerate(held):
                    span = slice(tile * BLOCK, (tile + 1) * BLOCK)
                    packed = jnp.where(lane == 2 * place_in, tops[tile], packed)
                    packed = jnp.where(lane == 2 * place_in + 1, sums[span], packed)
                stat_out[index, group, tile] = jnp.transpose(packed)[:height]
            stat_copy(index, group).start()

        def host_source(index, which, parity=None, slot=None):
            def bias(tile):
                return guest_bias[2 * index + which, tile : tile + 1, :]

            if slot is not None:
                get_k, get_v, _ = in_slot(slot)
                return get_k, get_v, bias

            def own(ref):
                return lambda cols: jnp.concatenate(
                    [ref[pl.ds((2 * pick + parity) * BLOCK, BLOCK), cols] for pick in range(picks)], axis=0
                )

            return own(k_own), own(v_own), bias

        def merge(group):
            start, count = groups[group]
            result_copy(0, group).wait_recv()
            stat_copy(0, group).wait_recv()

            def one_tile(tile, carry):
                span = pl.ds(pl.multiple_of(tile * BLOCK, BLOCK), BLOCK)
                packed = jnp.concatenate(
                    [stat_in[group, tile], jnp.zeros((LANES - height, BLOCK), jnp.float32)], axis=0
                )
                stats = jnp.transpose(packed)
                for index in range(count):
                    head = start + index
                    their_top = jnp.broadcast_to(stats[:, 2 * index : 2 * index + 1], (BLOCK, HEAD))
                    their_sum = jnp.broadcast_to(stats[:, 2 * index + 1 : 2 * index + 2], (BLOCK, HEAD))
                    old_top = top[head, span, :]
                    new_top = jnp.maximum(old_top, their_top)
                    ours, theirs = jnp.exp2(old_top - new_top), jnp.exp2(their_top - new_top)
                    value = guest[0, span, columns(head, 1)].astype(jnp.float32)
                    top[head, span, :] = new_top
                    mixed[head, span, :] = mixed[head, span, :] * ours + value * theirs
                    total[head, span, :] = total[head, span, :] * ours + their_sum * theirs
                return carry

            lax.fori_loop(0, blocks, one_tile, 0)

        is_place = [place == role for role in range(4)]

        @pl.when(even)
        def _():
            pl.semaphore_wait(barrier, 3)
            pl.semaphore_signal(ready.at[0], inc=1, device_id=partner, device_id_type=MESH)

        @pl.when(is_place[0])
        def _():
            start_channel(0, 1)
            start_channel(0, 0)

        @pl.when(is_place[2])
        def _():
            for group in high:
                query_copy(1, group).start()
            start_channel(2, 0)

        @pl.when(odd)
        def _():
            pl.semaphore_wait(ready.at[0], 1)

        @pl.when(is_place[1])
        def _():
            for index in (1, 0, 2):
                start_channel(1, index)

        @pl.when(is_place[3])
        def _():
            start_channel(3, 1)
            start_channel(3, 0)

        fill()

        @pl.when(is_place[2])
        def _():
            for which in (0, 1):
                bias_copy(1, which).start()
            start_channel(2, 1)

        @pl.when(odd)
        def _():
            pl.semaphore_wait(barrier, expected)
            pl.semaphore_signal(ready.at[1], inc=1, device_id=partner, device_id_type=MESH)

        @pl.when(is_place[1])
        def _():
            start_channel(1, 3)

        @pl.when(is_place[3])
        def _():
            for group in every:
                query_copy(0, group).start()
            for which in (0, 1):
                bias_copy(0, which).start()

        @pl.when(even)
        def _():
            pl.semaphore_wait(ready.at[1], 1)

        start_halos()

        rows_wait()

        @pl.when(is_place[2])
        def _():
            start_channel(2, 2)

        @pl.when(is_place[3])
        def _():
            start_channel(3, 2)

        attend_own()

        beside = 1 - lax.rem(place, 2)
        band_wait(0, heads)

        @pl.when(is_place[3])
        def _():
            start_channel(3, 3)

        def relay(role, channel, slot, group):
            band_wait(landing(role, slot, members[group][0]), groups[group][1])
            start_channel(role, channel, members[group])

        @pl.when(is_place[1])
        def _():
            relay(1, 4, 3, 0)

        attend(*in_slot(beside), band_keys)

        @pl.when(is_place[0])
        def _():
            bias_wait(1).wait_recv()
            for group in high:
                query_copy(1, group).wait_recv()
                host(1, group, [host_source(1, 0, parity=1), host_source(1, 1, slot=1)])

        @pl.when(is_place[1])
        def _():
            relay(1, 4, 3, 1)

        attend_halos()

        @pl.when(is_place[0])
        def _():
            bias_wait(0).wait_recv()
            for group in every:
                relay(0, 2, 5, group)
                query_copy(0, group).wait_recv()
                band_wait(landing(0, 3, members[group][0]), groups[group][1])
                host(0, group, [host_source(0, 0, parity=0), host_source(0, 1, slot=3)])
            channels_sent(0, 0, 1)
            results_sent(1)

        @pl.when(is_place[1])
        def _():
            for group in every[2:]:
                relay(1, 4, 3, group)
            attend(*in_slot(3), band_keys)
            channels_sent(1, 0, 1, 3)

        @pl.when(is_place[2])
        def _():
            for slot in (2, 0):
                band_wait(landing(2, slot, 0), low_span[1])
            attend(*joined([in_slot(2), in_slot(0)]), 2 * band_keys, bounds=low_span)
            queries_sent(1)
            channels_sent(2, 0)

        @pl.when(is_place[3])
        def _():
            queries_sent(0)
            channels_sent(3, 0, 1)

        halos_sent()
        early_slot = jnp.where(is_place[3], 2, 5)
        late_slot = jnp.where(lax.rem(place, 2) == 0, 3, 1)

        def wait_early(group):
            @pl.when(place > 0)
            def _():
                band_wait(first_early + group, groups[group][1])

        def wait_late(part, kinds=2, apart=0):
            @pl.when(place > 0)
            def _():
                band_wait(first_late + part + apart, parts[part][1], kinds)

        def merge_there(group):
            @pl.when(is_place[3] | (is_place[2] if group in high else place < 0))
            def _():
                merge(group)

        get_k, get_v, get_bias = in_slot(late_slot)
        final_group = len(groups) - 1
        for group in every:
            if group == 0:
                merge_there(0)
                wait_early(final_group)
                attend(*in_slot(early_slot), band_keys, bounds=groups[final_group])
            if group < final_group:
                wait_early(group)
                for part in members[group]:
                    wait_late(part)
                    attend(
                        *joined([in_slot(early_slot), in_slot(late_slot)]), 2 * band_keys,
                        mode="final", bounds=parts[part],
                    )
                merge_there(group + 1)
                continue

            @pl.when(is_place[0])
            def _():
                results_sent(0)

            @pl.when(is_place[1])
            def _():
                channels_sent(1, 4)

            @pl.when(is_place[2])
            def _():
                channels_sent(2, 1)

            @pl.when(is_place[3])
            def _():
                channels_sent(3, 2, 3)

            for part in members[group]:
                last_part = part == final_spot

                def values(cols, part=part, last_part=last_part):
                    if last_part:
                        wait_late(part, kinds=1, apart=1)
                    return get_v(cols)

                wait_late(part, kinds=1 if last_part else 2)
                attend(get_k, values, get_bias, band_keys, mode="final", bounds=parts[part])

        for role, index in ((0, 2), (1, 2), (2, 2)):

            @pl.when(is_place[role])
            def _(role=role, index=index):
                channels_sent(role, index)


def shards(tm_count, space_count, queries, key_rows, value_rows, block_list, block_count):
    rows, width = queries.shape
    blocks = rows // BLOCK
    picks = blocks // 2
    heads = width // HEAD
    slots = 2 * (tm_count.bit_length() - 1)
    kind = key_rows.dtype
    groups, parts, _ = head_groups(heads)
    in_hbm = pl.BlockSpec(memory_space=pltpu.HBM)
    dma = pltpu.SemaphoreType.DMA
    scratch = [
        pltpu.SMEM(block_list.shape, block_list.dtype),
        pltpu.SMEM(block_count.shape, block_count.dtype),
        pltpu.VMEM((rows, width), kind),
        pltpu.VMEM((rows, width), kind),
        pltpu.VMEM((rows, width), kind),
        pltpu.VMEM((2, BLOCK, width), kind),
        pltpu.VMEM((2, BLOCK, width), kind),
        pltpu.VMEM((slots, picks, BLOCK, width), kind),
        pltpu.VMEM((slots, picks, BLOCK, width), kind),
        pltpu.VMEM((heads, rows, HEAD), jnp.float32),
        pltpu.VMEM((heads, rows, HEAD), jnp.float32),
        pltpu.VMEM((heads, rows, HEAD), jnp.float32),
        pltpu.VMEM((blocks, (blocks + 2) * BLOCK), jnp.float32),
        pltpu.VMEM((slots, blocks, picks * BLOCK), jnp.float32),
        dma((3,)),
        dma((2,)),
        dma((2,)),
        dma((max(7, slots),)),
        dma((landing_count(groups, parts, slots),)),
    ]
    if is_folded(tm_count):
        height = stat_height(heads)
        scratch += [
            pltpu.VMEM((2, rows, width), kind),
            pltpu.VMEM((2, rows, width), kind),
            pltpu.VMEM((4, blocks, picks * BLOCK), jnp.float32),
            pltpu.VMEM((2, len(groups), blocks, height, BLOCK), jnp.float32),
            pltpu.VMEM((len(groups), blocks, height, BLOCK), jnp.float32),
            pltpu.SemaphoreType.REGULAR((2,)),
        ]
    return pl.pallas_call(
        functools.partial(kernel, tm_count, space_count, block_list.shape[1]),
        out_shape=jax.ShapeDtypeStruct((rows, width), queries.dtype),
        in_specs=[in_hbm] * 5,
        out_specs=pl.BlockSpec(memory_space=pltpu.VMEM),
        scratch_shapes=scratch,
        compiler_params=pltpu.CompilerParams(
            collective_id=0, has_side_effects=True, vmem_limit_bytes=50 * 1024 * 1024
        ),
    )(*[
        pltpu.with_memory_space_constraint(array, pltpu.HBM)
        for array in (queries, key_rows, value_rows, block_list, block_count)
    ])


def solution(mesh):
    placed = (
        P(("tm", "space"), None),
        P(("tm", "space"), None),
        P(("tm", "space"), None),
        P(("tm", "space"), None),
        P(("tm", "space")),
    )
    return jax.shard_map(
        functools.partial(shards, mesh.shape["tm"], mesh.shape["space"]),
        mesh=mesh, in_specs=placed, out_specs=P(("tm", "space"), None), check_vma=False,
    )
```

```python
import functools
import math

import jax
import jax.numpy as jnp
from jax import lax
from jax.experimental import pallas as pl
from jax.experimental.pallas import tpu as pltpu
from jax.sharding import PartitionSpec as P

HEAD = 128
BLOCK = 128
LANES = 128
DEAD = -1e30
MESH = pl.DeviceIdType.MESH

def head_groups(heads):
    quarter = max(1, heads // 4)
    groups = [(start, min(quarter, heads - start)) for start in range(0, heads, quarter)]
    parts, members = [], []
    for index, (start, count) in enumerate(groups):
        pieces = [(start, count)] if index < len(groups) - 1 else [(start + i, 1) for i in range(count)]
        members.append(list(range(len(parts), len(parts) + len(pieces))))
        parts += pieces
    return groups, parts, members


def stat_height(heads):
    return -(-2 * max(count for _, count in head_groups(heads)[0]) // 8) * 8


def landing_count(groups, parts, slots):
    return max(slots, 2 + len(parts) + 3 * len(groups))


def is_folded(tm_count):
    return tm_count.bit_length() - 1 == 3


def kernel(
    tm_count, space_count, list_width,
    q_hbm, k_hbm, v_hbm, list_hbm, count_hbm, o_ref,
    list_ref, count_ref,
    q_own, k_own, v_own, k_halo, v_halo, k_band, v_band,
    top, total, mixed, near_bias, band_bias,
    local_sem, halo_send, halo_recv, sent, landed,
    *guests,
):
    rows, width = q_hbm.shape
    blocks = rows // BLOCK
    picks = blocks // 2
    band_keys = picks * BLOCK
    heads = width // HEAD
    bits = tm_count.bit_length() - 1
    folded = is_folded(tm_count)
    groups, parts, members = head_groups(heads)
    all_parts = list(range(len(parts)))
    frame = lax.axis_index("tm")
    slab = lax.axis_index("space")
    scale = math.log2(math.e) / HEAD**0.5
    early = frame < tm_count // 2 if folded else frame >= 0
    place = jnp.where(early, frame, tm_count - 1 - frame)
    step = jnp.where(early, 1, -1)

    def flag(pred):
        return jnp.where(pred, 1, 0)

    def at(spot):
        return {"tm": jnp.where(early, spot, tm_count - 1 - spot)}

    def exists(delta):
        return (frame + delta >= 0) & (frame + delta < tm_count)

    def slab_exists(delta):
        return (slab + delta >= 0) & (slab + delta < space_count)

    def remote(src, dst, send_sem, recv_sem, device):
        return pltpu.make_async_remote_copy(
            src_ref=src, dst_ref=dst, send_sem=send_sem, recv_sem=recv_sem,
            device_id=device, device_id_type=MESH,
        )

    barrier = pltpu.get_barrier_semaphore()

    def greet(pred, device):
        @pl.when(pred)
        def _():
            pl.semaphore_signal(barrier, inc=1, device_id=device, device_id_type=MESH)

    hub = lax.rem(frame, 2) == 1
    outer = place < 2
    side_of_hub = jnp.where(early, 1, 0)
    partner = at(place + 1 - 2 * lax.rem(place, 2))
    expected = 0
    if folded:
        greet(outer, at(2 + side_of_hub))
        greet(jnp.logical_not(outer), at(side_of_hub))
        greet(jnp.logical_not(hub), partner)
        greet(outer, at(5 - side_of_hub))
        greet(jnp.logical_not(outer), at(7 - side_of_hub))
        expected = 2
        listener = at(jnp.where(outer, 0, 2) + 1 - side_of_hub)
        for delta in (-1, 1):
            greet(slab_exists(delta), {"space": slab + delta, **listener})
            expected = expected + 2 * flag(slab_exists(delta))
    else:
        for delta in (-1, 1):
            expected = expected + flag(slab_exists(delta))
            greet(slab_exists(delta), {"space": slab + delta})
        for bit in range(bits):
            for delta in (1 << bit, -(1 << bit)):
                expected = expected + flag(exists(delta))
                greet(exists(delta), {"tm": frame + delta})

    def halo_copies(side, delta):
        start = (blocks - 1) * BLOCK if side == 0 else 0
        for src, dst in ((k_hbm, k_halo), (v_hbm, v_halo)):
            yield remote(
                src.at[pl.ds(start, BLOCK)], dst.at[side],
                halo_send.at[side], halo_recv.at[side], {"space": slab + delta},
            )

    def halo_wait(side, delta):
        return remote(k_halo, k_halo, halo_send.at[side], halo_recv.at[side], {"space": slab + delta})

    def columns(start, count):
        return pl.ds(start * HEAD, count * HEAD)

    whole = [(0, 0, heads)]
    group_pieces = [(members[i][0], *group) for i, group in enumerate(groups)]
    part_pieces = [(i, *part) for i, part in enumerate(parts)]

    def own_band(ref, parity):
        return ref.reshape(picks, 2, BLOCK, width).at[:, parity]

    first_early, first_late = 1, 1 + len(groups)
    first_extra = first_late + len(parts) + 1
    final_spot = len(parts) - 1

    def landing(role, slot, spot):
        group = [index for index, some in enumerate(members) if spot in some][0]
        if not folded:
            return slot
        if slot == 1 - role % 2:
            return 0
        if slot == (2 if role == 3 else 5):
            return first_early + group
        if slot == (1 if role % 2 else 3):
            return first_late + spot
        return first_extra + (group if role == 1 else 1 if slot == 0 else 0)

    def band_copies(channel, source, slot, pieces, device, role=None):
        kind, which = source
        for spot, start, count in pieces:
            cols = columns(start, count)
            for index, (own, near, band) in enumerate(((k_hbm, k_own, k_band), (v_hbm, v_own, v_band))):
                src = band.at[which] if kind == "band" else own_band(own if kind == "own" else near, which)
                apart = index if spot == final_spot else 0
                yield remote(
                    src.at[:, :, cols], band.at[slot].at[:, :, cols],
                    sent.at[channel], landed.at[landing(role, slot, spot) + apart], device,
                )

    def band_bytes(channel, where, count, kinds=2):
        some = k_band.at[pl.ds(0, kinds), :, :, columns(0, count)]
        return remote(some, some, sent.at[channel], landed.at[where], {"tm": frame})

    def band_wait(where, count, kinds=2):
        band_bytes(0, where, count, kinds).wait_recv()

    def sent_wait(channel, pieces):
        band_bytes(channel, 0, sum(piece[2] for piece in pieces)).wait_send()

    local = [
        pltpu.make_async_copy(src, dst, local_sem.at[index])
        for index, src, dst in (
            (0, list_hbm, list_ref), (1, count_hbm, count_ref),
            (2, q_hbm, q_own), (2, k_hbm, k_own), (2, v_hbm, v_own),
        )
    ]
    for copy in local:
        copy.start()

    def rows_wait():
        all_three = k_band.at[pl.ds(0, 6)]
        pltpu.make_async_copy(all_three, all_three, local_sem.at[2]).wait()

    def start_halos():
        for side, delta in ((0, 1), (1, -1)):

            @pl.when(slab_exists(delta))
            def _(side=side, delta=delta):
                for copy in halo_copies(side, delta):
                    copy.start()

    def halos_sent():
        for side, delta in ((0, 1), (1, -1)):

            @pl.when(slab_exists(delta))
            def _(side=side, delta=delta):
                halo_wait(side, delta).wait_send()

    frame_blocks = blocks * space_count
    first_block = frame * frame_blocks + slab * blocks

    def bias_rows(ids):
        row = jnp.concatenate([jnp.full((1, BLOCK), ident, jnp.int32) for ident in ids], axis=1)
        out = []
        for tile in range(blocks):
            count = count_ref[tile]
            value = jnp.full(row.shape, DEAD, jnp.float32)
            for entry in range(list_width):
                listed = jnp.where(entry < count, list_ref[tile, entry], -1)
                value = jnp.where(row == listed, 0.0, value)
            out.append(value)
        return out

    def fill_bias():
        for bit in range(bits):
            for side in (0, 1):
                partner = frame + (2 * side - 1) * step * (1 << bit)
                ids = [
                    partner * frame_blocks + slab * blocks + 2 * pick + bit % 2
                    for pick in range(picks)
                ]
                for tile, value in enumerate(bias_rows(ids)):
                    band_bias[2 * bit + side, tile : tile + 1, :] = value

    def fill_near():
        near_ids = [first_block + c for c in range(blocks)] + [first_block - 1, first_block + blocks]
        for tile, value in enumerate(bias_rows(near_ids)):
            near_bias[tile : tile + 1, :] = value

    def attend(get_k, get_v, get_bias, keys, mode="add", bounds=None, get_q=None, export=None):
        ones = jnp.ones((keys, HEAD), jnp.bfloat16)
        queries = get_q or (lambda cols: q_own[:, cols])

        def one_head(head, carry):
            cols = pl.ds(pl.multiple_of(head * HEAD, HEAD), HEAD)
            raw = lax.dot_general(
                queries(cols), get_k(cols), (((1,), (1,)), ((), ())),
                preferred_element_type=jnp.float32,
            )
            weights, shrink, tops = [], [], []
            for tile in range(blocks):
                span = slice(tile * BLOCK, (tile + 1) * BLOCK)
                scores = raw[span] * scale + get_bias(tile)
                peak = jnp.max(scores, axis=1, keepdims=True)
                if mode in ("first", "export"):
                    new_top = jnp.broadcast_to(peak, (BLOCK, HEAD))
                else:
                    old_top = top[head, span, :]
                    new_top = jnp.maximum(old_top, peak)
                    shrink.append(jnp.exp2(old_top - new_top))
                if mode in ("first", "add"):
                    top[head, span, :] = new_top
                tops.append(new_top)
                wide = jnp.concatenate([new_top] * (keys // HEAD), axis=1)
                weights.append(jnp.exp2(scores - wide).astype(jnp.bfloat16))
            extended = jnp.concatenate([get_v(cols), ones], axis=1)
            both = jnp.dot(
                jnp.concatenate(weights, axis=0), extended, preferred_element_type=jnp.float32
            )
            if mode == "export":
                export(head, cols, both[:, :HEAD], tops, both[:, HEAD:])
            elif mode == "first":
                mixed[head] = both[:, :HEAD]
                total[head] = both[:, HEAD:]
            else:
                factor = jnp.concatenate(shrink, axis=0)
                new_mixed = mixed[head] * factor + both[:, :HEAD]
                new_total = total[head] * factor + both[:, HEAD:]
                if mode == "final":
                    o_ref[:, cols] = (new_mixed / new_total).astype(o_ref.dtype)
                else:
                    mixed[head] = new_mixed
                    total[head] = new_total
            return carry

        start, count = (0, heads) if bounds is None else bounds
        paired = count - count % 2
        if export is not None:
            paired = 0
        if paired > 2:
            lax.fori_loop(start, start + paired, one_head, 0, unroll=2)
        for head in range(start if paired <= 2 else start + paired, start + count):
            one_head(head, 0)

    def attend_own():
        attend(
            lambda cols: k_own[:, cols],
            lambda cols: v_own[:, cols],
            lambda tile: near_bias[tile : tile + 1, : blocks * BLOCK],
            blocks * BLOCK,
            mode="first",
        )

    def attend_halos():
        for side, delta in ((0, -1), (1, 1)):

            @pl.when(slab_exists(delta))
            def _(side=side, delta=delta):
                halo_wait(side, delta).wait_recv()
                start = (blocks + side) * BLOCK
                attend(
                    lambda cols: k_halo[side, :, cols],
                    lambda cols: v_halo[side, :, cols],
                    lambda tile: near_bias[tile : tile + 1, start : start + BLOCK],
                    BLOCK,
                )

    def in_slot(slot):
        return (
            lambda cols: k_band[slot, :, :, cols].reshape(band_keys, HEAD),
            lambda cols: v_band[slot, :, :, cols].reshape(band_keys, HEAD),
            lambda tile: band_bias[slot, tile : tile + 1, :],
        )

    def joined(sources):
        def join(index, axis):
            return lambda arg: jnp.concatenate([s[index](arg) for s in sources], axis=axis)

        return join(0, 0), join(1, 0), join(2, 1)

    def fill():
        for copy in local[:2]:
            copy.wait()
        fill_bias()
        fill_near()

    if not folded:
        fill()
        pl.semaphore_wait(barrier, expected)
        start_halos()
        for bit in list(range(1, bits)) + [0]:
            for side, delta in ((0, 1 << bit), (1, -(1 << bit))):

                @pl.when(exists(delta))
                def _(bit=bit, side=side, delta=delta):
                    slot = 2 * bit + side
                    for copy in band_copies(slot, ("own", bit % 2), slot, whole, {"tm": frame + delta}):
                        copy.start()

        rows_wait()
        attend_own()
        attend_halos()
        for bit in list(range(1, bits)) + [0]:
            for side, delta in ((0, -(1 << bit)), (1, 1 << bit)):

                @pl.when(exists(delta))
                def _(bit=bit, side=side):
                    slot = 2 * bit + side
                    band_wait(slot, heads)
                    attend(*in_slot(slot), band_keys)

        def finish(head, carry):
            cols = pl.ds(pl.multiple_of(head * HEAD, HEAD), HEAD)
            o_ref[:, cols] = (mixed[head] / total[head]).astype(o_ref.dtype)
            return carry

        lax.fori_loop(0, heads, finish, 0)
        for bit in range(bits):
            for side, delta in ((0, 1 << bit), (1, -(1 << bit))):

                @pl.when(exists(delta))
                def _(slot=2 * bit + side):
                    sent_wait(slot, whole)

        halos_sent()

    else:
        (
            guest, away, guest_bias, stat_out, stat_in, ready,
        ) = guests
        first_guest_sent, first_stat_sent = 3, 5
        query_sent, bias_sent = 4, 5
        upper = len(groups) // 2
        every, high = range(len(groups)), range(upper, len(groups))
        low_pieces = group_pieces[:upper]
        low_span = (0, groups[upper][0])

        channels = {
            0: [
                (("own", 0), 1, 0, whole),
                (("own", 1), 2, 2, low_pieces),
                (("band", 5), 3, 1, part_pieces),
            ],
            1: [
                (("own", 0), 0, 1, whole),
                (("own", 0), 2, 0, low_pieces),
                (("own", 1), 3, 2, group_pieces),
                (("own", 0), 5, 5, group_pieces),
                (("band", 3), 5, 3, part_pieces),
            ],
            2: [
                (("own", 0), 3, 0, whole),
                (("own", 1), 0, 3, group_pieces),
                (("near", 0), 1, 1, part_pieces),
            ],
            3: [
                (("own", 0), 2, 1, whole),
                (("own", 1), 1, 3, group_pieces),
                (("near", 0), 7, 5, group_pieces),
                (("band", 0), 6, 5, group_pieces),
            ],
        }

        def start_channel(role, index, spots=None):
            source, target, slot, pieces = channels[role][index]
            pieces = [piece for piece in pieces if spots is None or piece[0] in spots]
            role_there = min(target, tm_count - 1 - target)
            for copy in band_copies(index, source, slot, pieces, at(target), role_there):
                copy.start()

        def channels_sent(role, *indices):
            for index in indices:
                sent_wait(index, channels[role][index][3])

        guest_groups = (every, high)
        guest_host = (7, 0)
        guest_home = (4, 2)
        guest_slots = ((5, 3), (2, 0))

        def query_landing(index, group):
            return first_extra + group + (0 if index == 0 else len(groups) - upper)

        def query_copy(index, group):
            cols = columns(*groups[group])
            return remote(
                q_hbm.at[:, cols], guest.at[index, :, cols],
                sent.at[query_sent], landed.at[query_landing(index, group)], at(guest_host[index]),
            )

        def guest_wait_sent(index, channel):
            cols = columns(0, sum(groups[group][1] for group in guest_groups[index]))
            ref = guest.at[index, :, cols]
            remote(ref, ref, sent.at[channel], landed.at[0], {"tm": frame}).wait_send()

        def bias_landing(index):
            return first_extra + 2 * len(groups) - 2 + index

        def bias_copy(index, which):
            return remote(
                band_bias.at[guest_slots[index][which]], guest_bias.at[2 * index + which],
                sent.at[bias_sent], landed.at[bias_landing(index)], at(guest_host[index]),
            )

        def bias_wait(index):
            pair = guest_bias.at[pl.ds(2 * index, 2)]
            return remote(pair, pair, sent.at[bias_sent], landed.at[bias_landing(index)], {"tm": frame})

        def result_copy(index, group):
            cols = columns(*groups[group])
            return remote(
                away.at[index, :, cols], guest.at[0, :, cols],
                sent.at[first_guest_sent + index], landed.at[first_extra + group], at(guest_home[index]),
            )

        def stat_copy(index, group):
            return remote(
                stat_out.at[index, group], stat_in.at[group],
                sent.at[first_stat_sent + index], landed.at[first_extra + len(groups) + group],
                at(guest_home[index]),
            )

        def results_sent(index):
            guest_wait_sent(index, first_guest_sent + index)
            ref = stat_out.at[index, pl.ds(0, len(guest_groups[index]))]
            remote(ref, ref, sent.at[first_stat_sent + index], landed.at[0], {"tm": frame}).wait_send()

        def queries_sent(index):
            guest_wait_sent(index, query_sent)
            bias_wait(index).wait_send()

        height = stat_height(heads)

        def host(index, group, sources):
            held = []

            def export(head, cols, value, tops, sums):
                away[index, :, cols] = value.astype(away.dtype)
                held.append((tops, sums))

            attend(
                *joined(sources), 2 * band_keys, mode="export", bounds=groups[group],
                get_q=lambda cols: guest[index, :, cols], export=export,
            )
            result_copy(index, group).start()
            lane = lax.broadcasted_iota(jnp.int32, (BLOCK, LANES), 1)
            for tile in range(blocks):
                packed = jnp.zeros((BLOCK, LANES), jnp.float32)
                for place_in, (tops, sums) in enumerate(held):
                    span = slice(tile * BLOCK, (tile + 1) * BLOCK)
                    packed = jnp.where(lane == 2 * place_in, tops[tile], packed)
                    packed = jnp.where(lane == 2 * place_in + 1, sums[span], packed)
                stat_out[index, group, tile] = jnp.transpose(packed)[:height]
            stat_copy(index, group).start()

        def host_source(index, which, parity=None, slot=None):
            def bias(tile):
                return guest_bias[2 * index + which, tile : tile + 1, :]

            if slot is not None:
                get_k, get_v, _ = in_slot(slot)
                return get_k, get_v, bias

            def own(ref):
                return lambda cols: jnp.concatenate(
                    [ref[pl.ds((2 * pick + parity) * BLOCK, BLOCK), cols] for pick in range(picks)], axis=0
                )

            return own(k_own), own(v_own), bias

        def merge(group):
            start, count = groups[group]
            result_copy(0, group).wait_recv()
            stat_copy(0, group).wait_recv()

            def one_tile(tile, carry):
                span = pl.ds(pl.multiple_of(tile * BLOCK, BLOCK), BLOCK)
                packed = jnp.concatenate(
                    [stat_in[group, tile], jnp.zeros((LANES - height, BLOCK), jnp.float32)], axis=0
                )
                stats = jnp.transpose(packed)
                for index in range(count):
                    head = start + index
                    their_top = jnp.broadcast_to(stats[:, 2 * index : 2 * index + 1], (BLOCK, HEAD))
                    their_sum = jnp.broadcast_to(stats[:, 2 * index + 1 : 2 * index + 2], (BLOCK, HEAD))
                    old_top = top[head, span, :]
                    new_top = jnp.maximum(old_top, their_top)
                    ours, theirs = jnp.exp2(old_top - new_top), jnp.exp2(their_top - new_top)
                    value = guest[0, span, columns(head, 1)].astype(jnp.float32)
                    top[head, span, :] = new_top
                    mixed[head, span, :] = mixed[head, span, :] * ours + value * theirs
                    total[head, span, :] = total[head, span, :] * ours + their_sum * theirs
                return carry

            lax.fori_loop(0, blocks, one_tile, 0)

        is_place = [place == role for role in range(4)]

        @pl.when(hub)
        def _():
            pl.semaphore_wait(barrier, 3)
            pl.semaphore_signal(ready.at[0], inc=1, device_id=partner, device_id_type=MESH)

        @pl.when(jnp.logical_not(hub))
        def _():
            pl.semaphore_wait(ready.at[0], 1)

        @pl.when(is_place[2])
        def _():
            for group in high:
                query_copy(1, group).start()
            start_channel(2, 0)

        @pl.when(is_place[3])
        def _():
            start_channel(3, 1)
            start_channel(3, 0)

        @pl.when(is_place[0])
        def _():
            start_channel(0, 1)
            start_channel(0, 0)

        @pl.when(is_place[1])
        def _():
            for index in (1, 0, 2):
                start_channel(1, index)

        fill()

        @pl.when(is_place[2])
        def _():
            for which in (0, 1):
                bias_copy(1, which).start()
            start_channel(2, 1)

        @pl.when(jnp.logical_not(hub))
        def _():
            pl.semaphore_wait(barrier, expected)
            pl.semaphore_signal(ready.at[1], inc=1, device_id=partner, device_id_type=MESH)

        @pl.when(hub)
        def _():
            pl.semaphore_wait(ready.at[1], 1)

        @pl.when(is_place[1])
        def _():
            start_channel(1, 3)

        @pl.when(is_place[3])
        def _():
            for group in every:
                query_copy(0, group).start()
            for which in (0, 1):
                bias_copy(0, which).start()

        start_halos()

        rows_wait()

        @pl.when(is_place[2])
        def _():
            start_channel(2, 2)

        @pl.when(is_place[3])
        def _():
            start_channel(3, 2)

        attend_own()

        beside = 1 - lax.rem(place, 2)
        band_wait(0, heads)

        @pl.when(is_place[3])
        def _():
            start_channel(3, 3)

        def relay(role, channel, slot, group):
            band_wait(landing(role, slot, members[group][0]), groups[group][1])
            start_channel(role, channel, members[group])

        @pl.when(is_place[1])
        def _():
            relay(1, 4, 3, 0)

        attend(*in_slot(beside), band_keys)

        @pl.when(is_place[0])
        def _():
            bias_wait(1).wait_recv()
            for group in high:
                query_copy(1, group).wait_recv()
                host(1, group, [host_source(1, 0, parity=1), host_source(1, 1, slot=1)])

        @pl.when(is_place[1])
        def _():
            relay(1, 4, 3, 1)

        attend_halos()

        @pl.when(is_place[0])
        def _():
            bias_wait(0).wait_recv()
            for group in every:
                relay(0, 2, 5, group)
                query_copy(0, group).wait_recv()
                band_wait(landing(0, 3, members[group][0]), groups[group][1])
                host(0, group, [host_source(0, 0, parity=0), host_source(0, 1, slot=3)])
            channels_sent(0, 0, 1)
            results_sent(1)

        @pl.when(is_place[1])
        def _():
            for group in every[2:]:
                relay(1, 4, 3, group)
            attend(*in_slot(3), band_keys)
            channels_sent(1, 0, 1, 3)

        @pl.when(is_place[2])
        def _():
            for slot in (2, 0):
                band_wait(landing(2, slot, 0), low_span[1])
            attend(*joined([in_slot(2), in_slot(0)]), 2 * band_keys, bounds=low_span)
            queries_sent(1)
            channels_sent(2, 0)

        @pl.when(is_place[3])
        def _():
            queries_sent(0)
            channels_sent(3, 0, 1)

        halos_sent()
        early_slot = jnp.where(is_place[3], 2, 5)
        late_slot = jnp.where(lax.rem(place, 2) == 0, 3, 1)

        def wait_early(group):
            @pl.when(place > 0)
            def _():
                band_wait(first_early + group, groups[group][1])

        def wait_late(part, kinds=2, apart=0):
            @pl.when(place > 0)
            def _():
                band_wait(first_late + part + apart, parts[part][1], kinds)

        def merge_there(group):
            @pl.when(is_place[3] | (is_place[2] if group in high else place < 0))
            def _():
                merge(group)

        get_k, get_v, get_bias = in_slot(late_slot)
        final_group = len(groups) - 1
        for group in every:
            if group == 0:
                merge_there(0)
                wait_early(final_group)
                attend(*in_slot(early_slot), band_keys, bounds=groups[final_group])
            if group < final_group:
                wait_early(group)
                for part in members[group]:
                    wait_late(part)
                    attend(
                        *joined([in_slot(early_slot), in_slot(late_slot)]), 2 * band_keys,
                        mode="final", bounds=parts[part],
                    )
                merge_there(group + 1)
                continue

            @pl.when(is_place[0])
            def _():
                results_sent(0)

            @pl.when(is_place[1])
            def _():
                channels_sent(1, 4)

            @pl.when(is_place[2])
            def _():
                channels_sent(2, 1)

            @pl.when(is_place[3])
            def _():
                channels_sent(3, 2, 3)

            for part in members[group]:
                last_part = part == final_spot

                def values(cols, part=part, last_part=last_part):
                    if last_part:
                        wait_late(part, kinds=1, apart=1)
                    return get_v(cols)

                wait_late(part, kinds=1 if last_part else 2)
                attend(get_k, values, get_bias, band_keys, mode="final", bounds=parts[part])

        for role, index in ((0, 2), (1, 2), (2, 2)):

            @pl.when(is_place[role])
            def _(role=role, index=index):
                channels_sent(role, index)


def shards(tm_count, space_count, queries, key_rows, value_rows, block_list, block_count):
    rows, width = queries.shape
    blocks = rows // BLOCK
    picks = blocks // 2
    heads = width // HEAD
    slots = 2 * (tm_count.bit_length() - 1)
    kind = key_rows.dtype
    groups, parts, _ = head_groups(heads)
    in_hbm = pl.BlockSpec(memory_space=pltpu.HBM)
    dma = pltpu.SemaphoreType.DMA
    scratch = [
        pltpu.SMEM(block_list.shape, block_list.dtype),
        pltpu.SMEM(block_count.shape, block_count.dtype),
        pltpu.VMEM((rows, width), kind),
        pltpu.VMEM((rows, width), kind),
        pltpu.VMEM((rows, width), kind),
        pltpu.VMEM((2, BLOCK, width), kind),
        pltpu.VMEM((2, BLOCK, width), kind),
        pltpu.VMEM((slots, picks, BLOCK, width), kind),
        pltpu.VMEM((slots, picks, BLOCK, width), kind),
        pltpu.VMEM((heads, rows, HEAD), jnp.float32),
        pltpu.VMEM((heads, rows, HEAD), jnp.float32),
        pltpu.VMEM((heads, rows, HEAD), jnp.float32),
        pltpu.VMEM((blocks, (blocks + 2) * BLOCK), jnp.float32),
        pltpu.VMEM((slots, blocks, picks * BLOCK), jnp.float32),
        dma((3,)),
        dma((2,)),
        dma((2,)),
        dma((max(7, slots),)),
        dma((landing_count(groups, parts, slots),)),
    ]
    if is_folded(tm_count):
        height = stat_height(heads)
        scratch += [
            pltpu.VMEM((2, rows, width), kind),
            pltpu.VMEM((2, rows, width), kind),
            pltpu.VMEM((4, blocks, picks * BLOCK), jnp.float32),
            pltpu.VMEM((2, len(groups), blocks, height, BLOCK), jnp.float32),
            pltpu.VMEM((len(groups), blocks, height, BLOCK), jnp.float32),
            pltpu.SemaphoreType.REGULAR((2,)),
        ]
    return pl.pallas_call(
        functools.partial(kernel, tm_count, space_count, block_list.shape[1]),
        out_shape=jax.ShapeDtypeStruct((rows, width), queries.dtype),
        in_specs=[in_hbm] * 5,
        out_specs=pl.BlockSpec(memory_space=pltpu.VMEM),
        scratch_shapes=scratch,
        compiler_params=pltpu.CompilerParams(
            collective_id=0, has_side_effects=True, vmem_limit_bytes=50 * 1024 * 1024
        ),
    )(*[
        pltpu.with_memory_space_constraint(array, pltpu.HBM)
        for array in (queries, key_rows, value_rows, block_list, block_count)
    ])


def solution(mesh):
    placed = (
        P(("tm", "space"), None),
        P(("tm", "space"), None),
        P(("tm", "space"), None),
        P(("tm", "space"), None),
        P(("tm", "space")),
    )
    return jax.shard_map(
        functools.partial(shards, mesh.shape["tm"], mesh.shape["space"]),
        mesh=mesh, in_specs=placed, out_specs=P(("tm", "space"), None), check_vma=False,
    )
```

```python
import functools
import math

import jax
import jax.numpy as jnp
from jax import lax
from jax.experimental import pallas as pl
from jax.experimental.pallas import tpu as pltpu
from jax.sharding import PartitionSpec as P

HEAD = 128
BLOCK = 128
LANES = 128
DEAD = -1e30
MESH = pl.DeviceIdType.MESH

def head_groups(heads):
    quarter = max(1, heads // 4)
    groups = [(start, min(quarter, heads - start)) for start in range(0, heads, quarter)]
    parts, members = [], []
    for index, (start, count) in enumerate(groups):
        pieces = [(start, count)] if index < len(groups) - 1 else [(start + i, 1) for i in range(count)]
        members.append(list(range(len(parts), len(parts) + len(pieces))))
        parts += pieces
    return groups, parts, members


def stat_height(heads, blocks):
    return -(-2 * blocks * max(count for _, count in head_groups(heads)[0]) // 8) * 8


def landing_count(groups, parts, slots):
    return max(slots, 2 + len(parts) + 3 * len(groups))


def is_folded(tm_count):
    return tm_count.bit_length() - 1 == 3


def kernel(
    tm_count, space_count, list_width,
    q_hbm, k_hbm, v_hbm, list_hbm, count_hbm, o_ref,
    list_ref, count_ref,
    q_own, k_own, v_own, k_halo, v_halo, k_band, v_band,
    top, total, mixed, near_bias, band_bias,
    local_sem, halo_send, halo_recv, sent, landed,
    *guests,
):
    rows, width = q_hbm.shape
    blocks = rows // BLOCK
    picks = blocks // 2
    band_keys = picks * BLOCK
    heads = width // HEAD
    bits = tm_count.bit_length() - 1
    folded = is_folded(tm_count)
    groups, parts, members = head_groups(heads)
    all_parts = list(range(len(parts)))
    frame = lax.axis_index("tm")
    slab = lax.axis_index("space")
    scale = math.log2(math.e) / HEAD**0.5
    early = frame < tm_count // 2 if folded else frame >= 0
    place = jnp.where(early, frame, tm_count - 1 - frame)
    step = jnp.where(early, 1, -1)

    def flag(pred):
        return jnp.where(pred, 1, 0)

    def at(spot):
        return {"tm": jnp.where(early, spot, tm_count - 1 - spot)}

    def exists(delta):
        return (frame + delta >= 0) & (frame + delta < tm_count)

    def slab_exists(delta):
        return (slab + delta >= 0) & (slab + delta < space_count)

    def remote(src, dst, send_sem, recv_sem, device):
        return pltpu.make_async_remote_copy(
            src_ref=src, dst_ref=dst, send_sem=send_sem, recv_sem=recv_sem,
            device_id=device, device_id_type=MESH,
        )

    barrier = pltpu.get_barrier_semaphore()

    def greet(pred, device):
        @pl.when(pred)
        def _():
            pl.semaphore_signal(barrier, inc=1, device_id=device, device_id_type=MESH)

    hub = lax.rem(frame, 2) == 1
    outer = place < 2
    side_of_hub = jnp.where(early, 1, 0)
    partner = at(place + 1 - 2 * lax.rem(place, 2))
    expected = 0
    if folded:
        greet(outer, at(2 + side_of_hub))
        greet(jnp.logical_not(outer), at(side_of_hub))
        greet(jnp.logical_not(hub), partner)
        greet(outer, at(5 - side_of_hub))
        greet(jnp.logical_not(outer), at(7 - side_of_hub))
        expected = 2
        listener = at(jnp.where(outer, 0, 2) + 1 - side_of_hub)
        for delta in (-1, 1):
            greet(slab_exists(delta), {"space": slab + delta, **listener})
            expected = expected + 2 * flag(slab_exists(delta))
    else:
        for delta in (-1, 1):
            expected = expected + flag(slab_exists(delta))
            greet(slab_exists(delta), {"space": slab + delta})
        for bit in range(bits):
            for delta in (1 << bit, -(1 << bit)):
                expected = expected + flag(exists(delta))
                greet(exists(delta), {"tm": frame + delta})

    def halo_copies(side, delta):
        start = (blocks - 1) * BLOCK if side == 0 else 0
        for src, dst in ((k_hbm, k_halo), (v_hbm, v_halo)):
            yield remote(
                src.at[pl.ds(start, BLOCK)], dst.at[side],
                halo_send.at[side], halo_recv.at[side], {"space": slab + delta},
            )

    def halo_wait(side, delta):
        return remote(k_halo, k_halo, halo_send.at[side], halo_recv.at[side], {"space": slab + delta})

    def columns(start, count):
        return pl.ds(start * HEAD, count * HEAD)

    whole = [(0, 0, heads)]
    group_pieces = [(members[i][0], *group) for i, group in enumerate(groups)]
    part_pieces = [(i, *part) for i, part in enumerate(parts)]

    def own_band(ref, parity):
        return ref.reshape(picks, 2, BLOCK, width).at[:, parity]

    first_early, first_late = 1, 1 + len(groups)
    first_extra = first_late + len(parts) + 1
    final_spot = len(parts) - 1

    def landing(role, slot, spot):
        group = [index for index, some in enumerate(members) if spot in some][0]
        if not folded:
            return slot
        if slot == 1 - role % 2:
            return 0
        if slot == (2 if role == 3 else 5):
            return first_early + group
        if slot == (1 if role % 2 else 3):
            return first_late + spot
        return first_extra + (group if role == 1 else 1 if slot == 0 else 0)

    def band_copies(channel, source, slot, pieces, device, role=None):
        kind, which = source
        for spot, start, count in pieces:
            cols = columns(start, count)
            for index, (own, near, band) in enumerate(((k_hbm, k_own, k_band), (v_hbm, v_own, v_band))):
                src = band.at[which] if kind == "band" else own_band(own if kind == "own" else near, which)
                apart = index if spot == final_spot else 0
                yield remote(
                    src.at[:, :, cols], band.at[slot].at[:, :, cols],
                    sent.at[channel], landed.at[landing(role, slot, spot) + apart], device,
                )

    def band_bytes(channel, where, count, kinds=2):
        some = k_band.at[pl.ds(0, kinds), :, :, columns(0, count)]
        return remote(some, some, sent.at[channel], landed.at[where], {"tm": frame})

    def band_wait(where, count, kinds=2):
        band_bytes(0, where, count, kinds).wait_recv()

    def sent_wait(channel, pieces):
        band_bytes(channel, 0, sum(piece[2] for piece in pieces)).wait_send()

    local = [
        pltpu.make_async_copy(src, dst, local_sem.at[index])
        for index, src, dst in (
            (0, list_hbm, list_ref), (1, count_hbm, count_ref),
            (2, q_hbm, q_own), (2, k_hbm, k_own), (2, v_hbm, v_own),
        )
    ]
    for copy in local:
        copy.start()

    def rows_wait():
        all_three = k_band.at[pl.ds(0, 6)]
        pltpu.make_async_copy(all_three, all_three, local_sem.at[2]).wait()

    def start_halos():
        for side, delta in ((0, 1), (1, -1)):

            @pl.when(slab_exists(delta))
            def _(side=side, delta=delta):
                for copy in halo_copies(side, delta):
                    copy.start()

    def halos_sent():
        for side, delta in ((0, 1), (1, -1)):

            @pl.when(slab_exists(delta))
            def _(side=side, delta=delta):
                halo_wait(side, delta).wait_send()

    frame_blocks = blocks * space_count
    first_block = frame * frame_blocks + slab * blocks

    def bias_rows(ids):
        row = jnp.concatenate([jnp.full((1, BLOCK), ident, jnp.int32) for ident in ids], axis=1)
        out = []
        for tile in range(blocks):
            count = count_ref[tile]
            value = jnp.full(row.shape, DEAD, jnp.float32)
            for entry in range(list_width):
                listed = jnp.where(entry < count, list_ref[tile, entry], -1)
                value = jnp.where(row == listed, 0.0, value)
            out.append(value)
        return out

    def fill_bias():
        for bit in range(bits):
            for side in (0, 1):
                partner = frame + (2 * side - 1) * step * (1 << bit)
                ids = [
                    partner * frame_blocks + slab * blocks + 2 * pick + bit % 2
                    for pick in range(picks)
                ]
                for tile, value in enumerate(bias_rows(ids)):
                    band_bias[2 * bit + side, tile : tile + 1, :] = value

    def fill_near():
        near_ids = [first_block + c for c in range(blocks)] + [first_block - 1, first_block + blocks]
        for tile, value in enumerate(bias_rows(near_ids)):
            near_bias[tile : tile + 1, :] = value

    def attend(get_k, get_v, get_bias, keys, mode="add", bounds=None, get_q=None, export=None):
        ones = jnp.ones((keys, HEAD), jnp.bfloat16)
        queries = get_q or (lambda cols: q_own[:, cols])

        def one_head(head, carry):
            cols = pl.ds(pl.multiple_of(head * HEAD, HEAD), HEAD)
            raw = lax.dot_general(
                queries(cols), get_k(cols), (((1,), (1,)), ((), ())),
                preferred_element_type=jnp.float32,
            )
            weights, shrink, tops = [], [], []
            for tile in range(blocks):
                span = slice(tile * BLOCK, (tile + 1) * BLOCK)
                scores = raw[span] * scale + get_bias(tile)
                peak = jnp.max(scores, axis=1, keepdims=True)
                if mode in ("first", "export"):
                    new_top = jnp.broadcast_to(peak, (BLOCK, HEAD))
                else:
                    old_top = top[head, span, :]
                    new_top = jnp.maximum(old_top, peak)
                    shrink.append(jnp.exp2(old_top - new_top))
                if mode in ("first", "add"):
                    top[head, span, :] = new_top
                tops.append(new_top)
                wide = jnp.concatenate([new_top] * (keys // HEAD), axis=1)
                weights.append(jnp.exp2(scores - wide).astype(jnp.bfloat16))
            extended = jnp.concatenate([get_v(cols), ones], axis=1)
            both = jnp.dot(
                jnp.concatenate(weights, axis=0), extended, preferred_element_type=jnp.float32
            )
            if mode == "export":
                export(head, cols, both[:, :HEAD], tops, both[:, HEAD:])
            elif mode == "first":
                mixed[head] = both[:, :HEAD]
                total[head] = both[:, HEAD:]
            else:
                factor = jnp.concatenate(shrink, axis=0)
                new_mixed = mixed[head] * factor + both[:, :HEAD]
                new_total = total[head] * factor + both[:, HEAD:]
                if mode == "final":
                    o_ref[:, cols] = (new_mixed / new_total).astype(o_ref.dtype)
                else:
                    mixed[head] = new_mixed
                    total[head] = new_total
            return carry

        start, count = (0, heads) if bounds is None else bounds
        paired = count - count % 2
        if export is not None:
            paired = 0
        if paired > 2:
            lax.fori_loop(start, start + paired, one_head, 0, unroll=2)
        for head in range(start if paired <= 2 else start + paired, start + count):
            one_head(head, 0)

    def attend_own():
        attend(
            lambda cols: k_own[:, cols],
            lambda cols: v_own[:, cols],
            lambda tile: near_bias[tile : tile + 1, : blocks * BLOCK],
            blocks * BLOCK,
            mode="first",
        )

    def attend_halos():
        for side, delta in ((0, -1), (1, 1)):

            @pl.when(slab_exists(delta))
            def _(side=side, delta=delta):
                halo_wait(side, delta).wait_recv()
                start = (blocks + side) * BLOCK
                attend(
                    lambda cols: k_halo[side, :, cols],
                    lambda cols: v_halo[side, :, cols],
                    lambda tile: near_bias[tile : tile + 1, start : start + BLOCK],
                    BLOCK,
                )

    def in_slot(slot):
        return (
            lambda cols: k_band[slot, :, :, cols].reshape(band_keys, HEAD),
            lambda cols: v_band[slot, :, :, cols].reshape(band_keys, HEAD),
            lambda tile: band_bias[slot, tile : tile + 1, :],
        )

    def joined(sources):
        def join(index, axis):
            return lambda arg: jnp.concatenate([s[index](arg) for s in sources], axis=axis)

        return join(0, 0), join(1, 0), join(2, 1)

    def fill():
        for copy in local[:2]:
            copy.wait()
        fill_bias()
        fill_near()

    if not folded:
        fill()
        pl.semaphore_wait(barrier, expected)
        start_halos()
        for bit in list(range(1, bits)) + [0]:
            for side, delta in ((0, 1 << bit), (1, -(1 << bit))):

                @pl.when(exists(delta))
                def _(bit=bit, side=side, delta=delta):
                    slot = 2 * bit + side
                    for copy in band_copies(slot, ("own", bit % 2), slot, whole, {"tm": frame + delta}):
                        copy.start()

        rows_wait()
        attend_own()
        attend_halos()
        for bit in list(range(1, bits)) + [0]:
            for side, delta in ((0, -(1 << bit)), (1, 1 << bit)):

                @pl.when(exists(delta))
                def _(bit=bit, side=side):
                    slot = 2 * bit + side
                    band_wait(slot, heads)
                    attend(*in_slot(slot), band_keys)

        def finish(head, carry):
            cols = pl.ds(pl.multiple_of(head * HEAD, HEAD), HEAD)
            o_ref[:, cols] = (mixed[head] / total[head]).astype(o_ref.dtype)
            return carry

        lax.fori_loop(0, heads, finish, 0)
        for bit in range(bits):
            for side, delta in ((0, 1 << bit), (1, -(1 << bit))):

                @pl.when(exists(delta))
                def _(slot=2 * bit + side):
                    sent_wait(slot, whole)

        halos_sent()

    else:
        (
            guest, away, guest_bias, stat_out, stat_in, ready,
        ) = guests
        first_guest_sent, first_stat_sent = 3, 5
        query_sent, bias_sent = 4, 5
        upper = len(groups) // 2
        every, high = range(len(groups)), range(upper, len(groups))
        low_pieces = group_pieces[:upper]
        low_span = (0, groups[upper][0])

        channels = {
            0: [
                (("own", 0), 1, 0, whole),
                (("own", 1), 2, 2, low_pieces),
                (("band", 5), 3, 1, part_pieces),
            ],
            1: [
                (("own", 0), 0, 1, whole),
                (("own", 0), 2, 0, low_pieces),
                (("own", 1), 3, 2, group_pieces),
                (("own", 0), 5, 5, group_pieces),
                (("band", 3), 5, 3, part_pieces),
            ],
            2: [
                (("own", 0), 3, 0, whole),
                (("own", 1), 0, 3, group_pieces),
                (("near", 0), 1, 1, part_pieces),
            ],
            3: [
                (("own", 0), 2, 1, whole),
                (("own", 1), 1, 3, group_pieces),
                (("near", 0), 7, 5, group_pieces),
                (("band", 0), 6, 5, group_pieces),
            ],
        }

        def start_channel(role, index, spots=None):
            source, target, slot, pieces = channels[role][index]
            pieces = [piece for piece in pieces if spots is None or piece[0] in spots]
            role_there = min(target, tm_count - 1 - target)
            for copy in band_copies(index, source, slot, pieces, at(target), role_there):
                copy.start()

        def channels_sent(role, *indices):
            for index in indices:
                sent_wait(index, channels[role][index][3])

        guest_groups = (every, high)
        guest_host = (7, 0)
        guest_home = (4, 2)
        guest_slots = ((5, 3), (2, 0))

        def query_landing(index, group):
            return first_extra + group + (0 if index == 0 else len(groups) - upper)

        def query_copy(index, group):
            cols = columns(*groups[group])
            return remote(
                q_hbm.at[:, cols], guest.at[index, :, cols],
                sent.at[query_sent], landed.at[query_landing(index, group)], at(guest_host[index]),
            )

        def guest_wait_sent(index, channel):
            cols = columns(0, sum(groups[group][1] for group in guest_groups[index]))
            ref = guest.at[index, :, cols]
            remote(ref, ref, sent.at[channel], landed.at[0], {"tm": frame}).wait_send()

        def bias_landing(index):
            return first_extra + 2 * len(groups) - 2 + index

        def bias_copy(index, which):
            return remote(
                band_bias.at[guest_slots[index][which]], guest_bias.at[2 * index + which],
                sent.at[bias_sent], landed.at[bias_landing(index)], at(guest_host[index]),
            )

        def bias_wait(index):
            pair = guest_bias.at[pl.ds(2 * index, 2)]
            return remote(pair, pair, sent.at[bias_sent], landed.at[bias_landing(index)], {"tm": frame})

        def result_copy(index, group):
            cols = columns(*groups[group])
            return remote(
                away.at[index, :, cols], guest.at[0, :, cols],
                sent.at[first_guest_sent + index], landed.at[first_extra + group], at(guest_home[index]),
            )

        def stat_copy(index, group):
            return remote(
                stat_out.at[index, group], stat_in.at[group],
                sent.at[first_stat_sent + index], landed.at[first_extra + len(groups) + group],
                at(guest_home[index]),
            )

        def results_sent(index):
            guest_wait_sent(index, first_guest_sent + index)
            ref = stat_out.at[index, pl.ds(0, len(guest_groups[index]))]
            remote(ref, ref, sent.at[first_stat_sent + index], landed.at[0], {"tm": frame}).wait_send()

        def queries_sent(index):
            guest_wait_sent(index, query_sent)
            bias_wait(index).wait_send()

        height = stat_height(heads, blocks)

        def stat_lane(tile, index, count):
            return 2 * (tile * count + index)

        def host(index, group, sources):
            held = []

            def export(head, cols, value, tops, sums):
                away[index, :, cols] = value.astype(away.dtype)
                held.append((tops, sums))

            attend(
                *joined(sources), 2 * band_keys, mode="export", bounds=groups[group],
                get_q=lambda cols: guest[index, :, cols], export=export,
            )
            result_copy(index, group).start()
            lane = lax.broadcasted_iota(jnp.int32, (BLOCK, LANES), 1)
            packed = jnp.zeros((BLOCK, LANES), jnp.float32)
            for tile in range(blocks):
                for spot, (tops, sums) in enumerate(held):
                    span = slice(tile * BLOCK, (tile + 1) * BLOCK)
                    first = stat_lane(tile, spot, len(held))
                    packed = jnp.where(lane == first, tops[tile], packed)
                    packed = jnp.where(lane == first + 1, sums[span], packed)
            stat_out[index, group] = jnp.transpose(packed)[:height]
            stat_copy(index, group).start()

        def host_source(index, which, parity=None, slot=None):
            def bias(tile):
                return guest_bias[2 * index + which, tile : tile + 1, :]

            if slot is not None:
                get_k, get_v, _ = in_slot(slot)
                return get_k, get_v, bias

            def own(ref):
                return lambda cols: jnp.concatenate(
                    [ref[pl.ds((2 * pick + parity) * BLOCK, BLOCK), cols] for pick in range(picks)], axis=0
                )

            return own(k_own), own(v_own), bias

        def merge(group):
            start, count = groups[group]
            result_copy(0, group).wait_recv()
            stat_copy(0, group).wait_recv()

            stats = jnp.transpose(jnp.concatenate(
                [stat_in[group], jnp.zeros((LANES - height, BLOCK), jnp.float32)], axis=0
            ))
            for tile in range(blocks):
                span = slice(tile * BLOCK, (tile + 1) * BLOCK)
                for index in range(count):
                    head = start + index
                    first = stat_lane(tile, index, count)
                    their_top = jnp.broadcast_to(stats[:, first : first + 1], (BLOCK, HEAD))
                    their_sum = jnp.broadcast_to(stats[:, first + 1 : first + 2], (BLOCK, HEAD))
                    old_top = top[head, span, :]
                    new_top = jnp.maximum(old_top, their_top)
                    ours, theirs = jnp.exp2(old_top - new_top), jnp.exp2(their_top - new_top)
                    value = guest[0, span, columns(head, 1)].astype(jnp.float32)
                    top[head, span, :] = new_top
                    mixed[head, span, :] = mixed[head, span, :] * ours + value * theirs
                    total[head, span, :] = total[head, span, :] * ours + their_sum * theirs

        is_place = [place == role for role in range(4)]

        @pl.when(hub)
        def _():
            pl.semaphore_wait(barrier, 3)
            pl.semaphore_signal(ready.at[0], inc=1, device_id=partner, device_id_type=MESH)

        @pl.when(jnp.logical_not(hub))
        def _():
            pl.semaphore_wait(ready.at[0], 1)

        @pl.when(is_place[2])
        def _():
            for group in high:
                query_copy(1, group).start()
            start_channel(2, 0)

        @pl.when(is_place[3])
        def _():
            start_channel(3, 1)
            start_channel(3, 0)

        @pl.when(is_place[0])
        def _():
            start_channel(0, 1)
            start_channel(0, 0)

        @pl.when(is_place[1])
        def _():
            for index in (1, 0, 2):
                start_channel(1, index)

        fill()

        @pl.when(is_place[2])
        def _():
            for which in (0, 1):
                bias_copy(1, which).start()
            start_channel(2, 1)

        @pl.when(jnp.logical_not(hub))
        def _():
            pl.semaphore_wait(barrier, expected)
            pl.semaphore_signal(ready.at[1], inc=1, device_id=partner, device_id_type=MESH)

        @pl.when(hub)
        def _():
            pl.semaphore_wait(ready.at[1], 1)

        @pl.when(is_place[1])
        def _():
            start_channel(1, 3)

        @pl.when(is_place[3])
        def _():
            for group in every:
                query_copy(0, group).start()
            for which in (0, 1):
                bias_copy(0, which).start()

        start_halos()

        rows_wait()

        @pl.when(is_place[2])
        def _():
            start_channel(2, 2)

        @pl.when(is_place[3])
        def _():
            start_channel(3, 2)

        attend_own()

        beside = 1 - lax.rem(place, 2)
        band_wait(0, heads)

        @pl.when(is_place[3])
        def _():
            start_channel(3, 3)

        def relay(role, channel, slot, group):
            band_wait(landing(role, slot, members[group][0]), groups[group][1])
            start_channel(role, channel, members[group])

        @pl.when(is_place[1])
        def _():
            relay(1, 4, 3, 0)

        attend(*in_slot(beside), band_keys)

        @pl.when(is_place[0])
        def _():
            bias_wait(1).wait_recv()
            for group in high:
                query_copy(1, group).wait_recv()
                host(1, group, [host_source(1, 0, parity=1), host_source(1, 1, slot=1)])

        @pl.when(is_place[1])
        def _():
            relay(1, 4, 3, 1)

        attend_halos()

        @pl.when(is_place[0])
        def _():
            bias_wait(0).wait_recv()
            for group in every:
                relay(0, 2, 5, group)
                query_copy(0, group).wait_recv()
                band_wait(landing(0, 3, members[group][0]), groups[group][1])
                host(0, group, [host_source(0, 0, parity=0), host_source(0, 1, slot=3)])
            channels_sent(0, 0, 1)
            results_sent(1)

        @pl.when(is_place[1])
        def _():
            for group in every[2:]:
                relay(1, 4, 3, group)
            attend(*in_slot(3), band_keys)
            channels_sent(1, 0, 1, 3)

        @pl.when(is_place[2])
        def _():
            for slot in (2, 0):
                band_wait(landing(2, slot, 0), low_span[1])
            attend(*joined([in_slot(2), in_slot(0)]), 2 * band_keys, bounds=low_span)
            queries_sent(1)
            channels_sent(2, 0)

        @pl.when(is_place[3])
        def _():
            queries_sent(0)
            channels_sent(3, 0, 1)

        halos_sent()
        early_slot = jnp.where(is_place[3], 2, 5)
        late_slot = jnp.where(lax.rem(place, 2) == 0, 3, 1)

        def wait_early(group):
            @pl.when(place > 0)
            def _():
                band_wait(first_early + group, groups[group][1])

        def wait_late(part, kinds=2, apart=0):
            @pl.when(place > 0)
            def _():
                band_wait(first_late + part + apart, parts[part][1], kinds)

        def merge_there(group):
            @pl.when(is_place[3] | (is_place[2] if group in high else place < 0))
            def _():
                merge(group)

        get_k, get_v, get_bias = in_slot(late_slot)
        final_group = len(groups) - 1
        for group in every:
            if group == 0:
                merge_there(0)
                wait_early(final_group)
                attend(*in_slot(early_slot), band_keys, bounds=groups[final_group])
            if group < final_group:
                wait_early(group)
                for part in members[group]:
                    wait_late(part)
                    attend(
                        *joined([in_slot(early_slot), in_slot(late_slot)]), 2 * band_keys,
                        mode="final", bounds=parts[part],
                    )
                merge_there(group + 1)
                continue

            @pl.when(is_place[0])
            def _():
                results_sent(0)

            @pl.when(is_place[1])
            def _():
                channels_sent(1, 4)

            @pl.when(is_place[2])
            def _():
                channels_sent(2, 1)

            @pl.when(is_place[3])
            def _():
                channels_sent(3, 2, 3)

            for part in members[group]:
                last_part = part == final_spot

                def values(cols, part=part, last_part=last_part):
                    if last_part:
                        wait_late(part, kinds=1, apart=1)
                    return get_v(cols)

                wait_late(part, kinds=1 if last_part else 2)
                attend(get_k, values, get_bias, band_keys, mode="final", bounds=parts[part])

        for role, index in ((0, 2), (1, 2), (2, 2)):

            @pl.when(is_place[role])
            def _(role=role, index=index):
                channels_sent(role, index)


def shards(tm_count, space_count, queries, key_rows, value_rows, block_list, block_count):
    rows, width = queries.shape
    blocks = rows // BLOCK
    picks = blocks // 2
    heads = width // HEAD
    slots = 2 * (tm_count.bit_length() - 1)
    kind = key_rows.dtype
    groups, parts, _ = head_groups(heads)
    in_hbm = pl.BlockSpec(memory_space=pltpu.HBM)
    dma = pltpu.SemaphoreType.DMA
    scratch = [
        pltpu.SMEM(block_list.shape, block_list.dtype),
        pltpu.SMEM(block_count.shape, block_count.dtype),
        pltpu.VMEM((rows, width), kind),
        pltpu.VMEM((rows, width), kind),
        pltpu.VMEM((rows, width), kind),
        pltpu.VMEM((2, BLOCK, width), kind),
        pltpu.VMEM((2, BLOCK, width), kind),
        pltpu.VMEM((slots, picks, BLOCK, width), kind),
        pltpu.VMEM((slots, picks, BLOCK, width), kind),
        pltpu.VMEM((heads, rows, HEAD), jnp.float32),
        pltpu.VMEM((heads, rows, HEAD), jnp.float32),
        pltpu.VMEM((heads, rows, HEAD), jnp.float32),
        pltpu.VMEM((blocks, (blocks + 2) * BLOCK), jnp.float32),
        pltpu.VMEM((slots, blocks, picks * BLOCK), jnp.float32),
        dma((3,)),
        dma((2,)),
        dma((2,)),
        dma((max(7, slots),)),
        dma((landing_count(groups, parts, slots),)),
    ]
    if is_folded(tm_count):
        height = stat_height(heads, blocks)
        scratch += [
            pltpu.VMEM((2, rows, width), kind),
            pltpu.VMEM((2, rows, width), kind),
            pltpu.VMEM((4, blocks, picks * BLOCK), jnp.float32),
            pltpu.VMEM((2, len(groups), height, BLOCK), jnp.float32),
            pltpu.VMEM((len(groups), height, BLOCK), jnp.float32),
            pltpu.SemaphoreType.REGULAR((2,)),
        ]
    return pl.pallas_call(
        functools.partial(kernel, tm_count, space_count, block_list.shape[1]),
        out_shape=jax.ShapeDtypeStruct((rows, width), queries.dtype),
        in_specs=[in_hbm] * 5,
        out_specs=pl.BlockSpec(memory_space=pltpu.VMEM),
        scratch_shapes=scratch,
        compiler_params=pltpu.CompilerParams(
            collective_id=0, has_side_effects=True, vmem_limit_bytes=50 * 1024 * 1024
        ),
    )(*[
        pltpu.with_memory_space_constraint(array, pltpu.HBM)
        for array in (queries, key_rows, value_rows, block_list, block_count)
    ])


def solution(mesh):
    placed = (
        P(("tm", "space"), None),
        P(("tm", "space"), None),
        P(("tm", "space"), None),
        P(("tm", "space"), None),
        P(("tm", "space")),
    )
    return jax.shard_map(
        functools.partial(shards, mesh.shape["tm"], mesh.shape["space"]),
        mesh=mesh, in_specs=placed, out_specs=P(("tm", "space"), None), check_vma=False,
    )
```

```python
import functools
import math

import jax
import jax.numpy as jnp
from jax import lax
from jax.experimental import pallas as pl
from jax.experimental.pallas import tpu as pltpu
from jax.sharding import PartitionSpec as P

HEAD = 128
BLOCK = 128
LANES = 128
DEAD = -1e30
MESH = pl.DeviceIdType.MESH

def head_groups(heads):
    quarter = max(1, heads // 4)
    groups = [(start, min(quarter, heads - start)) for start in range(0, heads, quarter)]
    parts, members = [], []
    for index, (start, count) in enumerate(groups):
        pieces = [(start, count)] if index < len(groups) - 1 else [(start + i, 1) for i in range(count)]
        members.append(list(range(len(parts), len(parts) + len(pieces))))
        parts += pieces
    return groups, parts, members


def stat_height(heads, blocks):
    return -(-2 * blocks * max(count for _, count in head_groups(heads)[0]) // 8) * 8


def landing_count(groups, parts, slots):
    return max(slots, 2 + len(parts) + 3 * len(groups))


def is_folded(tm_count):
    return tm_count.bit_length() - 1 == 3


def kernel(
    tm_count, space_count, list_width,
    q_hbm, k_hbm, v_hbm, list_hbm, count_hbm, o_ref,
    list_ref, count_ref,
    q_own, k_own, v_own, k_halo, v_halo, k_band, v_band,
    top, total, mixed, near_bias, band_bias,
    local_sem, halo_send, halo_recv, sent, landed,
    *guests,
):
    rows, width = q_hbm.shape
    blocks = rows // BLOCK
    picks = blocks // 2
    band_keys = picks * BLOCK
    heads = width // HEAD
    bits = tm_count.bit_length() - 1
    folded = is_folded(tm_count)
    groups, parts, members = head_groups(heads)
    all_parts = list(range(len(parts)))
    frame = lax.axis_index("tm")
    slab = lax.axis_index("space")
    scale = math.log2(math.e) / HEAD**0.5
    early = frame < tm_count // 2 if folded else frame >= 0
    place = jnp.where(early, frame, tm_count - 1 - frame)
    step = jnp.where(early, 1, -1)

    def flag(pred):
        return jnp.where(pred, 1, 0)

    def at(spot):
        return {"tm": jnp.where(early, spot, tm_count - 1 - spot)}

    def exists(delta):
        return (frame + delta >= 0) & (frame + delta < tm_count)

    def slab_exists(delta):
        return (slab + delta >= 0) & (slab + delta < space_count)

    def remote(src, dst, send_sem, recv_sem, device):
        return pltpu.make_async_remote_copy(
            src_ref=src, dst_ref=dst, send_sem=send_sem, recv_sem=recv_sem,
            device_id=device, device_id_type=MESH,
        )

    barrier = pltpu.get_barrier_semaphore()

    def greet(pred, device):
        @pl.when(pred)
        def _():
            pl.semaphore_signal(barrier, inc=1, device_id=device, device_id_type=MESH)

    hub = lax.rem(frame, 2) == 1
    outer = place < 2
    side_of_hub = jnp.where(early, 1, 0)
    partner = at(place + 1 - 2 * lax.rem(place, 2))
    expected = 0
    if folded:
        greet(outer, at(2 + side_of_hub))
        greet(jnp.logical_not(outer), at(side_of_hub))
        greet(jnp.logical_not(hub), partner)
        greet(outer, at(5 - side_of_hub))
        greet(jnp.logical_not(outer), at(7 - side_of_hub))
        expected = 2
        listener = at(jnp.where(outer, 0, 2) + 1 - side_of_hub)
        for delta in (-1, 1):
            greet(slab_exists(delta), {"space": slab + delta, **listener})
            expected = expected + 2 * flag(slab_exists(delta))
    else:
        for delta in (-1, 1):
            expected = expected + flag(slab_exists(delta))
            greet(slab_exists(delta), {"space": slab + delta})
        for bit in range(bits):
            for delta in (1 << bit, -(1 << bit)):
                expected = expected + flag(exists(delta))
                greet(exists(delta), {"tm": frame + delta})

    def halo_copies(side, delta):
        start = (blocks - 1) * BLOCK if side == 0 else 0
        for src, dst in ((k_hbm, k_halo), (v_hbm, v_halo)):
            yield remote(
                src.at[pl.ds(start, BLOCK)], dst.at[side],
                halo_send.at[side], halo_recv.at[side], {"space": slab + delta},
            )

    def halo_wait(side, delta):
        return remote(k_halo, k_halo, halo_send.at[side], halo_recv.at[side], {"space": slab + delta})

    def columns(start, count):
        return pl.ds(start * HEAD, count * HEAD)

    whole = [(0, 0, heads)]
    group_pieces = [(members[i][0], *group) for i, group in enumerate(groups)]
    part_pieces = [(i, *part) for i, part in enumerate(parts)]

    def own_band(ref, parity):
        return ref.reshape(picks, 2, BLOCK, width).at[:, parity]

    first_early, first_late = 1, 1 + len(groups)
    first_extra = first_late + len(parts) + 1
    final_spot = len(parts) - 1

    def landing(role, slot, spot):
        group = [index for index, some in enumerate(members) if spot in some][0]
        if not folded:
            return slot
        if slot == 1 - role % 2:
            return 0
        if slot == (2 if role == 3 else 5):
            return first_early + group
        if slot == (1 if role % 2 else 3):
            return first_late + spot
        return first_extra + (group if role == 1 else 1 if slot == 0 else 0)

    def band_copies(channel, source, slot, pieces, device, role=None):
        kind, which = source
        for spot, start, count in pieces:
            cols = columns(start, count)
            for index, (own, near, band) in enumerate(((k_hbm, k_own, k_band), (v_hbm, v_own, v_band))):
                src = band.at[which] if kind == "band" else own_band(own if kind == "own" else near, which)
                apart = index if spot == final_spot else 0
                yield remote(
                    src.at[:, :, cols], band.at[slot].at[:, :, cols],
                    sent.at[channel], landed.at[landing(role, slot, spot) + apart], device,
                )

    def band_bytes(channel, where, count, kinds=2):
        some = k_band.at[pl.ds(0, kinds), :, :, columns(0, count)]
        return remote(some, some, sent.at[channel], landed.at[where], {"tm": frame})

    def band_wait(where, count, kinds=2):
        band_bytes(0, where, count, kinds).wait_recv()

    def sent_wait(channel, pieces):
        band_bytes(channel, 0, sum(piece[2] for piece in pieces)).wait_send()

    local = [
        pltpu.make_async_copy(src, dst, local_sem.at[index])
        for index, src, dst in (
            (0, list_hbm, list_ref), (1, count_hbm, count_ref),
            (2, q_hbm, q_own), (2, k_hbm, k_own), (2, v_hbm, v_own),
        )
    ]
    for copy in local:
        copy.start()

    def rows_wait():
        all_three = k_band.at[pl.ds(0, 6)]
        pltpu.make_async_copy(all_three, all_three, local_sem.at[2]).wait()

    def start_halos():
        for side, delta in ((0, 1), (1, -1)):

            @pl.when(slab_exists(delta))
            def _(side=side, delta=delta):
                for copy in halo_copies(side, delta):
                    copy.start()

    def halos_sent():
        for side, delta in ((0, 1), (1, -1)):

            @pl.when(slab_exists(delta))
            def _(side=side, delta=delta):
                halo_wait(side, delta).wait_send()

    frame_blocks = blocks * space_count
    first_block = frame * frame_blocks + slab * blocks

    def bias_rows(ids):
        row = jnp.concatenate([jnp.full((1, BLOCK), ident, jnp.int32) for ident in ids], axis=1)
        out = []
        for tile in range(blocks):
            count = count_ref[tile]
            value = jnp.full(row.shape, DEAD, jnp.float32)
            for entry in range(list_width):
                listed = jnp.where(entry < count, list_ref[tile, entry], -1)
                value = jnp.where(row == listed, 0.0, value)
            out.append(value)
        return out

    def fill_bias():
        for bit in range(bits):
            for side in (0, 1):
                partner = frame + (2 * side - 1) * step * (1 << bit)
                ids = [
                    partner * frame_blocks + slab * blocks + 2 * pick + bit % 2
                    for pick in range(picks)
                ]
                for tile, value in enumerate(bias_rows(ids)):
                    band_bias[2 * bit + side, tile : tile + 1, :] = value

    def fill_near():
        near_ids = [first_block + c for c in range(blocks)] + [first_block - 1, first_block + blocks]
        for tile, value in enumerate(bias_rows(near_ids)):
            near_bias[tile : tile + 1, :] = value

    def attend(get_k, get_v, get_bias, keys, mode="add", bounds=None, get_q=None, export=None):
        ones = jnp.ones((keys, HEAD), jnp.bfloat16)
        queries = get_q or (lambda cols: q_own[:, cols])

        def one_head(head, carry):
            cols = pl.ds(pl.multiple_of(head * HEAD, HEAD), HEAD)
            raw = lax.dot_general(
                queries(cols), get_k(cols), (((1,), (1,)), ((), ())),
                preferred_element_type=jnp.float32,
            )
            weights, shrink, tops = [], [], []
            for tile in range(blocks):
                span = slice(tile * BLOCK, (tile + 1) * BLOCK)
                scores = raw[span] * scale + get_bias(tile)
                peak = jnp.max(scores, axis=1, keepdims=True)
                if mode in ("first", "export"):
                    new_top = jnp.broadcast_to(peak, (BLOCK, HEAD))
                else:
                    old_top = top[head, span, :]
                    new_top = jnp.maximum(old_top, peak)
                    shrink.append(jnp.exp2(old_top - new_top))
                if mode in ("first", "add"):
                    top[head, span, :] = new_top
                tops.append(new_top)
                wide = jnp.concatenate([new_top] * (keys // HEAD), axis=1)
                weights.append(jnp.exp2(scores - wide).astype(jnp.bfloat16))
            extended = jnp.concatenate([get_v(cols), ones], axis=1)
            both = jnp.dot(
                jnp.concatenate(weights, axis=0), extended, preferred_element_type=jnp.float32
            )
            if mode == "export":
                export(head, cols, both[:, :HEAD], tops, both[:, HEAD:])
            elif mode == "first":
                mixed[head] = both[:, :HEAD]
                total[head] = both[:, HEAD:]
            else:
                factor = jnp.concatenate(shrink, axis=0)
                new_mixed = mixed[head] * factor + both[:, :HEAD]
                new_total = total[head] * factor + both[:, HEAD:]
                if mode == "final":
                    o_ref[:, cols] = (new_mixed / new_total).astype(o_ref.dtype)
                else:
                    mixed[head] = new_mixed
                    total[head] = new_total
            return carry

        start, count = (0, heads) if bounds is None else bounds
        paired = count - count % 2
        if export is not None:
            paired = 0
        if paired > 2:
            lax.fori_loop(start, start + paired, one_head, 0, unroll=2)
        for head in range(start if paired <= 2 else start + paired, start + count):
            one_head(head, 0)

    def attend_own():
        attend(
            lambda cols: k_own[:, cols],
            lambda cols: v_own[:, cols],
            lambda tile: near_bias[tile : tile + 1, : blocks * BLOCK],
            blocks * BLOCK,
            mode="first",
        )

    def attend_halos():
        for side, delta in ((0, -1), (1, 1)):

            @pl.when(slab_exists(delta))
            def _(side=side, delta=delta):
                halo_wait(side, delta).wait_recv()
                start = (blocks + side) * BLOCK
                attend(
                    lambda cols: k_halo[side, :, cols],
                    lambda cols: v_halo[side, :, cols],
                    lambda tile: near_bias[tile : tile + 1, start : start + BLOCK],
                    BLOCK,
                )

    def in_slot(slot):
        return (
            lambda cols: k_band[slot, :, :, cols].reshape(band_keys, HEAD),
            lambda cols: v_band[slot, :, :, cols].reshape(band_keys, HEAD),
            lambda tile: band_bias[slot, tile : tile + 1, :],
        )

    def joined(sources):
        def join(index, axis):
            return lambda arg: jnp.concatenate([s[index](arg) for s in sources], axis=axis)

        return join(0, 0), join(1, 0), join(2, 1)

    def fill():
        for copy in local[:2]:
            copy.wait()
        fill_bias()

    if not folded:
        fill()
        fill_near()
        pl.semaphore_wait(barrier, expected)
        start_halos()
        for bit in list(range(1, bits)) + [0]:
            for side, delta in ((0, 1 << bit), (1, -(1 << bit))):

                @pl.when(exists(delta))
                def _(bit=bit, side=side, delta=delta):
                    slot = 2 * bit + side
                    for copy in band_copies(slot, ("own", bit % 2), slot, whole, {"tm": frame + delta}):
                        copy.start()

        rows_wait()
        attend_own()
        attend_halos()
        for bit in list(range(1, bits)) + [0]:
            for side, delta in ((0, -(1 << bit)), (1, 1 << bit)):

                @pl.when(exists(delta))
                def _(bit=bit, side=side):
                    slot = 2 * bit + side
                    band_wait(slot, heads)
                    attend(*in_slot(slot), band_keys)

        def finish(head, carry):
            cols = pl.ds(pl.multiple_of(head * HEAD, HEAD), HEAD)
            o_ref[:, cols] = (mixed[head] / total[head]).astype(o_ref.dtype)
            return carry

        lax.fori_loop(0, heads, finish, 0)
        for bit in range(bits):
            for side, delta in ((0, 1 << bit), (1, -(1 << bit))):

                @pl.when(exists(delta))
                def _(slot=2 * bit + side):
                    sent_wait(slot, whole)

        halos_sent()

    else:
        (
            guest, away, guest_bias, stat_out, stat_in, ready,
        ) = guests
        first_guest_sent, first_stat_sent = 3, 5
        query_sent, bias_sent = 4, 5
        upper = len(groups) // 2
        every, high = range(len(groups)), range(upper, len(groups))
        low_pieces = group_pieces[:upper]
        low_span = (0, groups[upper][0])

        channels = {
            0: [
                (("own", 0), 1, 0, whole),
                (("own", 1), 2, 2, low_pieces),
                (("band", 5), 3, 1, part_pieces),
            ],
            1: [
                (("own", 0), 0, 1, whole),
                (("own", 0), 2, 0, low_pieces),
                (("own", 1), 3, 2, group_pieces),
                (("own", 0), 5, 5, group_pieces),
                (("band", 3), 5, 3, part_pieces),
            ],
            2: [
                (("own", 0), 3, 0, whole),
                (("own", 1), 0, 3, group_pieces),
                (("near", 0), 1, 1, part_pieces),
            ],
            3: [
                (("own", 0), 2, 1, whole),
                (("own", 1), 1, 3, group_pieces),
                (("near", 0), 7, 5, group_pieces),
                (("band", 0), 6, 5, group_pieces),
            ],
        }

        def start_channel(role, index, spots=None):
            source, target, slot, pieces = channels[role][index]
            pieces = [piece for piece in pieces if spots is None or piece[0] in spots]
            role_there = min(target, tm_count - 1 - target)
            for copy in band_copies(index, source, slot, pieces, at(target), role_there):
                copy.start()

        def channels_sent(role, *indices):
            for index in indices:
                sent_wait(index, channels[role][index][3])

        guest_groups = (every, high)
        guest_host = (7, 0)
        guest_home = (4, 2)
        guest_slots = ((5, 3), (2, 0))

        def query_landing(index, group):
            return first_extra + group + (0 if index == 0 else len(groups) - upper)

        def query_copy(index, group):
            cols = columns(*groups[group])
            return remote(
                q_hbm.at[:, cols], guest.at[index, :, cols],
                sent.at[query_sent], landed.at[query_landing(index, group)], at(guest_host[index]),
            )

        def guest_wait_sent(index, channel):
            cols = columns(0, sum(groups[group][1] for group in guest_groups[index]))
            ref = guest.at[index, :, cols]
            remote(ref, ref, sent.at[channel], landed.at[0], {"tm": frame}).wait_send()

        def bias_landing(index):
            return first_extra + 2 * len(groups) - 2 + index

        def bias_copy(index, which):
            return remote(
                band_bias.at[guest_slots[index][which]], guest_bias.at[2 * index + which],
                sent.at[bias_sent], landed.at[bias_landing(index)], at(guest_host[index]),
            )

        def bias_wait(index):
            pair = guest_bias.at[pl.ds(2 * index, 2)]
            return remote(pair, pair, sent.at[bias_sent], landed.at[bias_landing(index)], {"tm": frame})

        def result_copy(index, group):
            cols = columns(*groups[group])
            return remote(
                away.at[index, :, cols], guest.at[0, :, cols],
                sent.at[first_guest_sent + index], landed.at[first_extra + group], at(guest_home[index]),
            )

        def stat_copy(index, group):
            return remote(
                stat_out.at[index, group], stat_in.at[group],
                sent.at[first_stat_sent + index], landed.at[first_extra + len(groups) + group],
                at(guest_home[index]),
            )

        def results_sent(index):
            guest_wait_sent(index, first_guest_sent + index)
            ref = stat_out.at[index, pl.ds(0, len(guest_groups[index]))]
            remote(ref, ref, sent.at[first_stat_sent + index], landed.at[0], {"tm": frame}).wait_send()

        def queries_sent(index):
            guest_wait_sent(index, query_sent)
            bias_wait(index).wait_send()

        height = stat_height(heads, blocks)

        def stat_lane(tile, index, count):
            return 2 * (tile * count + index)

        def host(index, group, sources):
            held = []

            def export(head, cols, value, tops, sums):
                away[index, :, cols] = value.astype(away.dtype)
                held.append((tops, sums))

            attend(
                *joined(sources), 2 * band_keys, mode="export", bounds=groups[group],
                get_q=lambda cols: guest[index, :, cols], export=export,
            )
            result_copy(index, group).start()
            lane = lax.broadcasted_iota(jnp.int32, (BLOCK, LANES), 1)
            packed = jnp.zeros((BLOCK, LANES), jnp.float32)
            for tile in range(blocks):
                for spot, (tops, sums) in enumerate(held):
                    span = slice(tile * BLOCK, (tile + 1) * BLOCK)
                    first = stat_lane(tile, spot, len(held))
                    packed = jnp.where(lane == first, tops[tile], packed)
                    packed = jnp.where(lane == first + 1, sums[span], packed)
            stat_out[index, group] = jnp.transpose(packed)[:height]
            stat_copy(index, group).start()

        def host_source(index, which, parity=None, slot=None):
            def bias(tile):
                return guest_bias[2 * index + which, tile : tile + 1, :]

            if slot is not None:
                get_k, get_v, _ = in_slot(slot)
                return get_k, get_v, bias

            def own(ref):
                return lambda cols: jnp.concatenate(
                    [ref[pl.ds((2 * pick + parity) * BLOCK, BLOCK), cols] for pick in range(picks)], axis=0
                )

            return own(k_own), own(v_own), bias

        def merge(group):
            start, count = groups[group]
            result_copy(0, group).wait_recv()
            stat_copy(0, group).wait_recv()

            stats = jnp.transpose(jnp.concatenate(
                [stat_in[group], jnp.zeros((LANES - height, BLOCK), jnp.float32)], axis=0
            ))
            for tile in range(blocks):
                span = slice(tile * BLOCK, (tile + 1) * BLOCK)
                for index in range(count):
                    head = start + index
                    first = stat_lane(tile, index, count)
                    their_top = jnp.broadcast_to(stats[:, first : first + 1], (BLOCK, HEAD))
                    their_sum = jnp.broadcast_to(stats[:, first + 1 : first + 2], (BLOCK, HEAD))
                    old_top = top[head, span, :]
                    new_top = jnp.maximum(old_top, their_top)
                    ours, theirs = jnp.exp2(old_top - new_top), jnp.exp2(their_top - new_top)
                    value = guest[0, span, columns(head, 1)].astype(jnp.float32)
                    top[head, span, :] = new_top
                    mixed[head, span, :] = mixed[head, span, :] * ours + value * theirs
                    total[head, span, :] = total[head, span, :] * ours + their_sum * theirs

        is_place = [place == role for role in range(4)]

        @pl.when(hub)
        def _():
            pl.semaphore_wait(barrier, 3)
            pl.semaphore_signal(ready.at[0], inc=1, device_id=partner, device_id_type=MESH)

        @pl.when(jnp.logical_not(hub))
        def _():
            pl.semaphore_wait(ready.at[0], 1)

        @pl.when(is_place[2])
        def _():
            for group in high:
                query_copy(1, group).start()
            start_channel(2, 0)

        @pl.when(is_place[3])
        def _():
            start_channel(3, 1)
            start_channel(3, 0)

        @pl.when(is_place[0])
        def _():
            start_channel(0, 1)
            start_channel(0, 0)

        @pl.when(is_place[1])
        def _():
            for index in (1, 0, 2):
                start_channel(1, index)

        fill()

        @pl.when(is_place[2])
        def _():
            for which in (0, 1):
                bias_copy(1, which).start()
            start_channel(2, 1)

        @pl.when(jnp.logical_not(hub))
        def _():
            pl.semaphore_wait(barrier, expected)
            pl.semaphore_signal(ready.at[1], inc=1, device_id=partner, device_id_type=MESH)

        @pl.when(hub)
        def _():
            pl.semaphore_wait(ready.at[1], 1)

        @pl.when(is_place[1])
        def _():
            start_channel(1, 3)

        @pl.when(is_place[3])
        def _():
            for group in every:
                query_copy(0, group).start()
            for which in (0, 1):
                bias_copy(0, which).start()

        start_halos()
        fill_near()
        rows_wait()

        @pl.when(is_place[2])
        def _():
            start_channel(2, 2)

        @pl.when(is_place[3])
        def _():
            start_channel(3, 2)

        attend_own()

        beside = 1 - lax.rem(place, 2)
        band_wait(0, heads)

        @pl.when(is_place[3])
        def _():
            start_channel(3, 3)

        def relay(role, channel, slot, group):
            band_wait(landing(role, slot, members[group][0]), groups[group][1])
            start_channel(role, channel, members[group])

        @pl.when(is_place[1])
        def _():
            relay(1, 4, 3, 0)

        attend(*in_slot(beside), band_keys)

        @pl.when(is_place[0])
        def _():
            bias_wait(1).wait_recv()
            for group in high:
                query_copy(1, group).wait_recv()
                host(1, group, [host_source(1, 0, parity=1), host_source(1, 1, slot=1)])

        @pl.when(is_place[1])
        def _():
            relay(1, 4, 3, 1)

        attend_halos()

        @pl.when(is_place[0])
        def _():
            bias_wait(0).wait_recv()
            for group in every:
                relay(0, 2, 5, group)
                query_copy(0, group).wait_recv()
                band_wait(landing(0, 3, members[group][0]), groups[group][1])
                host(0, group, [host_source(0, 0, parity=0), host_source(0, 1, slot=3)])
            channels_sent(0, 0, 1)
            results_sent(1)

        @pl.when(is_place[1])
        def _():
            for group in every[2:]:
                relay(1, 4, 3, group)
            attend(*in_slot(3), band_keys)
            channels_sent(1, 0, 1, 3)

        @pl.when(is_place[2])
        def _():
            for slot in (2, 0):
                band_wait(landing(2, slot, 0), low_span[1])
            attend(*joined([in_slot(2), in_slot(0)]), 2 * band_keys, bounds=low_span)
            queries_sent(1)
            channels_sent(2, 0)

        @pl.when(is_place[3])
        def _():
            queries_sent(0)
            channels_sent(3, 0, 1)

        halos_sent()
        early_slot = jnp.where(is_place[3], 2, 5)
        late_slot = jnp.where(lax.rem(place, 2) == 0, 3, 1)

        def wait_early(group):
            @pl.when(place > 0)
            def _():
                band_wait(first_early + group, groups[group][1])

        def wait_late(part, kinds=2, apart=0):
            @pl.when(place > 0)
            def _():
                band_wait(first_late + part + apart, parts[part][1], kinds)

        def merge_there(group):
            @pl.when(is_place[3] | (is_place[2] if group in high else place < 0))
            def _():
                merge(group)

        get_k, get_v, get_bias = in_slot(late_slot)
        final_group = len(groups) - 1
        for group in every:
            if group == 0:
                merge_there(0)
                wait_early(final_group)
                attend(*in_slot(early_slot), band_keys, bounds=groups[final_group])
            if group < final_group:
                wait_early(group)
                for part in members[group]:
                    wait_late(part)
                    attend(
                        *joined([in_slot(early_slot), in_slot(late_slot)]), 2 * band_keys,
                        mode="final", bounds=parts[part],
                    )
                merge_there(group + 1)
                continue

            @pl.when(is_place[0])
            def _():
                results_sent(0)

            @pl.when(is_place[1])
            def _():
                channels_sent(1, 4)

            @pl.when(is_place[2])
            def _():
                channels_sent(2, 1)

            @pl.when(is_place[3])
            def _():
                channels_sent(3, 2, 3)

            for part in members[group]:
                last_part = part == final_spot

                def values(cols, part=part, last_part=last_part):
                    if last_part:
                        wait_late(part, kinds=1, apart=1)
                    return get_v(cols)

                wait_late(part, kinds=1 if last_part else 2)
                attend(get_k, values, get_bias, band_keys, mode="final", bounds=parts[part])

        for role, index in ((0, 2), (1, 2), (2, 2)):

            @pl.when(is_place[role])
            def _(role=role, index=index):
                channels_sent(role, index)


def shards(tm_count, space_count, queries, key_rows, value_rows, block_list, block_count):
    rows, width = queries.shape
    blocks = rows // BLOCK
    picks = blocks // 2
    heads = width // HEAD
    slots = 2 * (tm_count.bit_length() - 1)
    kind = key_rows.dtype
    groups, parts, _ = head_groups(heads)
    in_hbm = pl.BlockSpec(memory_space=pltpu.HBM)
    dma = pltpu.SemaphoreType.DMA
    scratch = [
        pltpu.SMEM(block_list.shape, block_list.dtype),
        pltpu.SMEM(block_count.shape, block_count.dtype),
        pltpu.VMEM((rows, width), kind),
        pltpu.VMEM((rows, width), kind),
        pltpu.VMEM((rows, width), kind),
        pltpu.VMEM((2, BLOCK, width), kind),
        pltpu.VMEM((2, BLOCK, width), kind),
        pltpu.VMEM((slots, picks, BLOCK, width), kind),
        pltpu.VMEM((slots, picks, BLOCK, width), kind),
        pltpu.VMEM((heads, rows, HEAD), jnp.float32),
        pltpu.VMEM((heads, rows, HEAD), jnp.float32),
        pltpu.VMEM((heads, rows, HEAD), jnp.float32),
        pltpu.VMEM((blocks, (blocks + 2) * BLOCK), jnp.float32),
        pltpu.VMEM((slots, blocks, picks * BLOCK), jnp.float32),
        dma((3,)),
        dma((2,)),
        dma((2,)),
        dma((max(7, slots),)),
        dma((landing_count(groups, parts, slots),)),
    ]
    if is_folded(tm_count):
        height = stat_height(heads, blocks)
        scratch += [
            pltpu.VMEM((2, rows, width), kind),
            pltpu.VMEM((2, rows, width), kind),
            pltpu.VMEM((4, blocks, picks * BLOCK), jnp.float32),
            pltpu.VMEM((2, len(groups), height, BLOCK), jnp.float32),
            pltpu.VMEM((len(groups), height, BLOCK), jnp.float32),
            pltpu.SemaphoreType.REGULAR((2,)),
        ]
    return pl.pallas_call(
        functools.partial(kernel, tm_count, space_count, block_list.shape[1]),
        out_shape=jax.ShapeDtypeStruct((rows, width), queries.dtype),
        in_specs=[in_hbm] * 5,
        out_specs=pl.BlockSpec(memory_space=pltpu.VMEM),
        scratch_shapes=scratch,
        compiler_params=pltpu.CompilerParams(
            collective_id=0, has_side_effects=True, vmem_limit_bytes=50 * 1024 * 1024
        ),
    )(*[
        pltpu.with_memory_space_constraint(array, pltpu.HBM)
        for array in (queries, key_rows, value_rows, block_list, block_count)
    ])


def solution(mesh):
    placed = (
        P(("tm", "space"), None),
        P(("tm", "space"), None),
        P(("tm", "space"), None),
        P(("tm", "space"), None),
        P(("tm", "space")),
    )
    return jax.shard_map(
        functools.partial(shards, mesh.shape["tm"], mesh.shape["space"]),
        mesh=mesh, in_specs=placed, out_specs=P(("tm", "space"), None), check_vma=False,
    )
```
